32 devices in a mesh: row: 4 (over y, core), col: 8 (over z, x).
Axes of the slice: x: 2, y: 2, z: 4, core: 2. Of those that a mesh axis runs over, the one named last changes fastest.
Arguments:
- adjoint_field: float32 [5, 6, 192, 3072], P(None, None, 'row', 'col'), may hold values from -6 to 6
- advect_x: float32 [6, 192, 3072], P(None, 'row', 'col'), may hold values from -0.8 to 0.8
- advect_y: float32 [6, 192, 3072], P(None, 'row', 'col'), may hold values from -0.8 to 0.8
- diffusion: float32 [5, 6, 192, 3072], P(None, None, 'row', 'col'), may hold values from 0.02 to 0.2
- zone_cells: int32 [4], replicated, may hold values from 2 to 6
- feedback_dest: int32 [8, 64, 1], P('col', 'row'), may hold values from 0 to 7; in each aligned block of 16 rows (0 to 15, 16 to 31, ..., all dimensions but the last counted through in order) at most 2 rows name the same one
- feedback_slot: int32 [8, 64, 1], P('col', 'row'), may hold values from 0 to 79
Outputs:
- nest_adjoint: float32 [5, 6, 192, 3072], P(None, None, 'row', 'col')
- parent_adjoint: float32 [5, 6, 320, 1024], P(None, None, 'row', 'col')
The draws below stay inside these ranges and needn't reach their ends.
Inputs may be any that keep to these rules, and one draw needn't show every extreme that they name: `feedback_dest`: the 16 feedback rows of one device name one destination at most 2 times, a bound that some block reaches.
All inputs are finite; a program needn't handle non-finite values.
Results may differ from the reference program's by a relative error of at most 0.00012.
Values sent between devices are 32-bit elements; how exact they have to be, the bound alone decides.
A program may use at most 192 MiB of HBM per device.

```python
import math
import jax
import jax.numpy as jnp
import numpy as np
from jax import lax

F = 5
L = 6
ITERS = 3
PROWS = 80
CXC = 16
CYC = 128
CAP = 2
NX = 192
NY = 3072
NXC = 64
NYC = 1024
NPR = 320
N_COL = 8


def plant(values, rng, low, largest):
    spot = [jax.random.randint(jax.random.fold_in(rng, axis), (), 0, length) for axis, length in enumerate(values.shape)]
    main_axis = values.shape.index(max(values.shape))
    neighbour = spot[:main_axis] + [(spot[main_axis] + 1) % values.shape[main_axis]] + spot[main_axis + 1:]
    return values.at[tuple(spot)].set(low).at[tuple(neighbour)].set(largest)


def shard_levels(key, extent, cuts, low, top_value):
    gain, own = 1.0, jax.random.fold_in(key, 6)
    for dim, blocks in cuts:
        draws = jnp.exp(jax.random.uniform(jax.random.fold_in(own, dim), (blocks,), jnp.float32, low / len(cuts), top_value / len(cuts)))
        gain = gain * jnp.repeat(draws, extent[dim] // blocks).reshape([-1 if axis == dim else 1 for axis in range(len(extent))])
    return gain


def routed_block(stream_key, own, number, rows, amount, top, bound, lean):
    order = jax.random.permutation(stream_key, amount)
    crowded, ordinary = load_shares(amount, rows * top, bound, lean, True), load_shares(amount, rows * top, bound, lean, False)
    places = jnp.arange(amount)

    def named(tallies, turn):
        used = int((tallies > 0).sum())
        fixed = max(1, used // 4)
        shifted = fixed + (places - fixed + turn * (used - fixed)) % max(1, amount - fixed)
        return jnp.zeros((amount,), jnp.int32).at[order[jnp.where(places < fixed, places, shifted)]].set(jnp.asarray(tallies, jnp.int32))

    tallies = jnp.where(number % 4 == 0, named(crowded, number // 4), named(ordinary, number - number // 4 - 1))
    mixed = jax.random.permutation(jax.random.fold_in(own, 3), amount)
    source_of, taker = mixed[0:amount // 2 * 2:2], mixed[1:amount // 2 * 2:2]
    room = jnp.minimum(tallies[source_of] - 1, bound - tallies[taker]) // 2
    room = jnp.where((source_of == order[0]) | (taker == order[0]) | (tallies[taker] == 0), 0, jnp.maximum(room, 0))
    shifted = jax.random.randint(jax.random.fold_in(own, 4), (amount // 2,), 0, 1 << 20) % (room + 1)
    tallies = tallies.at[source_of].add(-shifted).at[taker].add(shifted)
    labels = jnp.searchsorted(jnp.cumsum(tallies), jnp.arange(rows * top), side="right").astype(jnp.int32)
    table = labels.reshape(top, rows).T
    table = table[jax.random.permutation(jax.random.fold_in(own, 1), rows)]
    turn = jax.random.randint(jax.random.fold_in(own, 2), (rows, 1), 0, top)
    return jnp.take_along_axis(table, (jnp.arange(top)[None, :] + turn) % top, axis=1)


def load_shares(number_of, total, bound, skew, full):
    portions = [(1 << 20) // math.isqrt(standing ** skew) + 1 for standing in range(1, number_of + 1)]
    largest = bound if full else min(bound, max(-(-total // number_of), total * portions[0] // sum(portions)))
    least = 1 if total - largest >= number_of - 1 else 0
    counts, rest = [largest] + [least] * (number_of - 1), total - largest - least * (number_of - 1)
    while rest > 0:
        movable = [i for i in range(1, number_of) if counts[i] < largest] or [i for i in range(1, number_of) if counts[i] < bound]
        mass, budget = sum([portions[i] for i in movable]), rest
        for i in movable:
            extra = min(bound - counts[i], max(1, budget * portions[i] // mass), rest)
            counts[i] = counts[i] + extra
            rest = rest - extra
    return np.array(counts)


def centred(stream_key, extent, deviation, reach, shards=(), kind=jnp.bfloat16):
    loudness = shard_levels(stream_key, extent, shards, -0.22, 0.18) if shards else 1.0
    entries = jax.random.normal(stream_key, extent, jnp.float32) * deviation * loudness
    return jnp.minimum(jnp.maximum(entries, -reach), reach).astype(kind)


def setup_inputs(seed: int = 0) -> dict:
    streams_of = jax.random.split(jax.random.key(seed), 8)
    adjoint_field = centred(streams_of[0], (F, L, NX, NY), 1.0, 6.0, ((2, 4), (3, 8)), jnp.float32)
    advect_x = jnp.clip(jax.random.uniform(streams_of[1], (L, NX, NY), jnp.float32, -0.8, 0.8) * shard_levels(streams_of[1], (L, NX, NY), ((1, 4), (2, 8)), -0.4, 0.0), -0.8, 0.8)
    advect_y = jnp.clip(jax.random.uniform(streams_of[2], (L, NX, NY), jnp.float32, -0.8, 0.8) * shard_levels(streams_of[2], (L, NX, NY), ((1, 4), (2, 8)), -0.4, 0.0), -0.8, 0.8)
    diffusion = jnp.clip(jnp.exp(math.log(0.2) - 2.3025851 * jax.random.uniform(streams_of[3], (F, L, NX, NY), jnp.float32) ** shard_levels(streams_of[3], (F, L, NX, NY), ((2, 4), (3, 8)), -0.2, 0.2)), 0.02, 0.2)
    zone_cells = plant(jax.random.randint(streams_of[4], (4,), 2, 7), jax.random.fold_in(streams_of[4], 1), 2, 6).astype(jnp.int32)
    feedback_dest_keys = jax.random.split(jax.random.fold_in(streams_of[5], 1), N_COL * NXC // CXC)
    feedback_dest_turns = jax.random.permutation(jax.random.fold_in(streams_of[5], 3), N_COL * NXC // CXC)
    feedback_dest = jax.vmap(lambda own, number: routed_block(jax.random.fold_in(streams_of[5], 2), own, number, CXC, N_COL, 1, CAP, 2))(feedback_dest_keys, feedback_dest_turns).reshape((N_COL, NXC, 1))
    feedback_slot = plant(jax.random.randint(streams_of[6], (N_COL, NXC, 1), 0, PROWS), jax.random.fold_in(streams_of[6], 1), 0, PROWS - 1).astype(jnp.int32)
    return {"adjoint_field": adjoint_field, "advect_x": advect_x, "advect_y": advect_y, "diffusion": diffusion, "zone_cells": zone_cells, "feedback_dest": feedback_dest, "feedback_slot": feedback_slot}


def advance(widened, coef_x, coef_y, coef_d):
    flux_x = coef_x * widened
    flux_y = coef_y * widened
    spread = coef_d * widened
    center = widened[..., 1:-1, 1:-1]
    result = center + 0.5 * (flux_x[..., 2:, 1:-1] - flux_x[..., :-2, 1:-1])
    result = result + 0.5 * (flux_y[..., 1:-1, 2:] - flux_y[..., 1:-1, :-2])
    result = result + spread[..., 2:, 1:-1] + spread[..., :-2, 1:-1]
    result = result + spread[..., 1:-1, 2:] + spread[..., 1:-1, :-2]
    return result - 4.0 * spread[..., 1:-1, 1:-1]


def ramp_weight(offset, count, total, low_zone, high_zone):
    positions = offset + jnp.arange(count, dtype=jnp.int32)
    lower = jnp.maximum(low_zone - positions, 0).astype(jnp.float32) / (low_zone + 1).astype(jnp.float32)
    upper = jnp.maximum(high_zone - (total - 1 - positions), 0).astype(jnp.float32) / (high_zone + 1).astype(jnp.float32)
    return jnp.maximum(lower, upper)


def reference(adjoint_field, advect_x, advect_y, diffusion, zone_cells, feedback_dest, feedback_slot):
    cycle = ((0, 0), (1, 1), (1, 1))
    padded_x = jnp.pad(advect_x, cycle)
    padded_y = jnp.pad(advect_y, cycle)

    def per_field(pair):
        field_now, spread_coef = pair
        padded_d = jnp.pad(spread_coef, cycle)
        for sweep in range(ITERS):
            field_now = advance(jnp.pad(field_now, cycle), padded_x, padded_y, padded_d)
        return field_now

    final = lax.map(per_field, (adjoint_field, diffusion))
    weight_rows = ramp_weight(0, NX, NX, zone_cells[0], zone_cells[1])
    weight_cols = ramp_weight(0, NY, NY, zone_cells[2], zone_cells[3])
    relaxation = jnp.maximum(weight_rows[:, None], weight_cols[None, :])
    nest_adjoint = (1.0 - relaxation) * final
    weighting = (1.0 - relaxation) / 9.0 + relaxation
    coarse = (weighting * final).reshape(F, L, NXC, 3, NYC, 3).sum(axis=(3, 5))
    blocks = coarse.reshape(F, L, NXC, N_COL, CYC)
    target_rows = (jnp.arange(NXC, dtype=jnp.int32) // CXC)[:, None] * PROWS + feedback_slot[:, :, 0].T
    target_cols = feedback_dest[:, :, 0].T
    parent = jnp.zeros((F, L, NPR, N_COL, CYC), jnp.float32).at[:, :, target_rows, target_cols].add(blocks)
    return nest_adjoint, parent.reshape(F, L, NPR, NYC)
```

```python
import functools

import jax
import jax.numpy as jnp
from jax import lax
from jax.experimental import pallas as pl
from jax.experimental.pallas import tpu as pltpu
from jax.sharding import PartitionSpec as P

ITERS = 3
PROWS = 80
CAP = 2
LANES = 128
SUB = 8
PACK = 4
SLOTS = LANES // PACK
CHUNK = 9
MESH = pl.DeviceIdType.MESH
DIRS = ((-1, 0), (1, 0), (0, 1), (0, -1), (-1, 1), (-1, -1), (1, 1), (1, -1))
NORTH, SOUTH, EAST, WEST, NE, NW, SE, SW = range(8)
OPPOSITE = (SOUTH, NORTH, WEST, EAST, SW, SE, NW, NE)
GREETED = (NORTH, SOUTH, NE, NW, SE, SW)


def round_up(value, step):
    return -(-value // step) * step


def split(values):
    high = values.astype(jnp.bfloat16)
    return high, (values - high.astype(jnp.float32)).astype(jnp.bfloat16)


def dot(left, right):
    return jnp.dot(left, right, preferred_element_type=jnp.float32)


def level_runs(levels, lead):
    runs, slot = [], 0
    while slot < levels + SUB - 1:
        level = (slot - lead) % levels
        count = min(levels - level, levels + SUB - 1 - slot)
        runs.append((slot, level, count))
        slot += count
    return runs


def kernel(
    dims,
    zone_ref,
    dest_ref,
    slot_ref,
    field_hbm,
    spread_hbm,
    along_x_hbm,
    along_y_hbm,
    nest,
    arrived,
    field,
    spread,
    along_x,
    along_y,
    ramps,
    keep,
    weigh,
    sums,
    pick,
    route,
    tags,
    outbound,
    rows_n,
    rows_s,
    got_n,
    got_s,
    slab_e,
    slab_w,
    got_e,
    got_w,
    corner_n,
    corner_s,
    got_corner,
    halo_coef,
    edge_coef,
    edges,
    load_sem,
    send_sem,
    recv_sem,
    out_sem,
    in_sem,
):
    fields, levels, tile_rows, tiles = dims
    planes = fields * levels
    padded = round_up(planes + 1, SUB)
    groups, lead = padded // SUB, padded - planes
    wide = tiles * SUB
    per = 2 * ITERS * wide
    row, col = lax.axis_index("row"), lax.axis_index("col")
    nrow, ncol = lax.axis_size("row"), lax.axis_size("col")
    coarse_rows = tile_rows // 3

    def exists(way):
        down, over = DIRS[way]
        conditions = []
        if down < 0:
            conditions.append(row > 0)
        if down > 0:
            conditions.append(row < nrow - 1)
        if over < 0:
            conditions.append(col > 0)
        if over > 0:
            conditions.append(col < ncol - 1)
        return functools.reduce(jnp.logical_and, conditions)

    def device(way):
        return (row + DIRS[way][0], col + DIRS[way][1])

    loads = [[] for _ in range(groups)]

    def load(group, source, source_row, target, target_row, count):
        for t in range(tiles):
            number = sum(len(some) for some in loads)
            copy = pltpu.make_async_copy(
                source.at[source_row : source_row + count, t * LANES : (t + 1) * LANES],
                target.at[t, target_row : target_row + count, :],
                load_sem.at[number],
            )
            copy.start()
            loads[group].append(copy)

    def load_group(group):
        low = max(group * SUB - lead, 0)
        high = (group + 1) * SUB - lead
        for source, target in ((field_hbm, field), (spread_hbm, spread)):
            load(
                group,
                source,
                low * tile_rows,
                target,
                (low + lead) * tile_rows,
                (high - low) * tile_rows,
            )

    load_group(0)
    for slot, level, count in level_runs(levels, lead):
        for source, target in ((along_x_hbm, along_x), (along_y_hbm, along_y)):
            load(0, source, level * tile_rows, target, slot * tile_rows, count * tile_rows)

    barrier = pltpu.get_barrier_semaphore()
    for way in GREETED:

        @pl.when(exists(way))
        def _(way=way):
            pl.semaphore_signal(barrier, inc=1, device_id=device(way), device_id_type=MESH)

    for step in range(1, ncol):
        pl.semaphore_signal(
            barrier, inc=1, device_id=(row, lax.rem(col + step, ncol)), device_id_type=MESH
        )

    for group in range(1, groups):
        load_group(group)

    lane = lax.broadcasted_iota(jnp.int32, (SUB, LANES), 1)
    block = lane // PACK
    lane_wide = lax.broadcasted_iota(jnp.int32, (wide, LANES), 1)
    lane_pair = lax.broadcasted_iota(jnp.int32, (2 * SUB, LANES), 1)
    inner = lane_pair % PACK

    for t in range(tiles):
        for ref in (field, spread):
            ref[t, 0 : lead * tile_rows, :] = jnp.zeros((lead * tile_rows, LANES), jnp.float32)

    def ramp(position, count, low_zone, high_zone):
        shape = position.shape
        scale_low = jnp.full(shape, (low_zone + 1).astype(jnp.float32))
        scale_high = jnp.full(shape, (high_zone + 1).astype(jnp.float32))
        lower = jnp.maximum(low_zone - position, 0).astype(jnp.float32) / scale_low
        upper = jnp.maximum(high_zone - (count - 1 - position), 0).astype(jnp.float32) / scale_high
        return jnp.maximum(lower, upper)

    row_index = row * tile_rows + lax.broadcasted_iota(jnp.int32, (tile_rows, LANES), 0)
    ramps[...] = ramp(row_index, tile_rows * nrow, zone_ref[0], zone_ref[1])
    tile_index = lax.broadcasted_iota(jnp.int32, (wide, LANES), 0) // SUB
    weight_cols = ramp(
        (col * tiles + tile_index) * LANES + lane_wide,
        tiles * LANES * ncol,
        zone_ref[2],
        zone_ref[3],
    )

    def weights(r, _):
        across = jnp.broadcast_to(ramps[pl.ds(r, 1), :], (wide, LANES))
        relaxation = jnp.maximum(across, weight_cols)
        at = pl.multiple_of(r * wide, SUB)
        keep[pl.ds(at, wide), :] = 1.0 - relaxation
        weigh[pl.ds(at, wide), :] = (1.0 - relaxation) / 9.0 + relaxation
        return 0

    lax.fori_loop(0, tile_rows, weights, 0, unroll=4)

    fine = lax.broadcasted_iota(jnp.int32, (tiles * LANES, LANES), 0)
    name = lax.broadcasted_iota(jnp.int32, (tiles * LANES, LANES), 1)
    pick[...] = (fine // 3 == name).astype(jnp.float32).astype(jnp.bfloat16)

    dests = [dest_ref[g] for g in range(coarse_rows)]
    from_lane = lax.broadcasted_iota(jnp.int32, (SUB, coarse_rows * SUB), 1)
    spot = jnp.zeros((SUB, coarse_rows * SUB), jnp.int32)
    for g in range(coarse_rows):
        rank = jnp.int32(0)
        for before in range(g):
            rank = rank + jnp.where(dests[before] == dests[g], 1, 0)
        spot = jnp.where(from_lane // SUB == g, dests[g] * CAP + rank, spot)
        tags[g * SUB : (g + 1) * SUB, :] = jnp.full(
            (SUB, LANES), (slot_ref[g] + 1).astype(jnp.float32)
        )
    same = from_lane % SUB == lax.broadcasted_iota(jnp.int32, (SUB, coarse_rows * SUB), 0)
    spot = jnp.where(same, spot, -1)
    for k in range(0, ncol * CAP, 2):
        pair = jnp.concatenate(
            [(spot == k).astype(jnp.float32), (spot == k + 1).astype(jnp.float32)], 0
        )
        route[k * SUB : (k + 2) * SUB, :] = pair.astype(jnp.bfloat16)

    received = {NORTH: got_n, SOUTH: got_s, EAST: got_e, WEST: got_w}
    for place, way in enumerate((NE, NW, SE, SW)):
        received[way] = got_corner.at[place]
    for way in range(8):

        @pl.when(jnp.logical_not(exists(way)))
        def _(way=way):
            received[way][...] = jnp.zeros(received[way].shape, jnp.float32)

    def planes_at(ref, t, group, r, count=padded):
        start = group * (SUB * tile_rows) + r
        return ref[t, pl.ds(start, SUB, stride=tile_rows), :]

    def gather_rows(source, group, at):
        for i in range(ITERS):
            for t in range(tiles):
                place = slice(at + i * wide + t * SUB, at + i * wide + (t + 1) * SUB)
                rows_n[place, :] = planes_at(source, t, group, i)
                rows_s[place, :] = planes_at(source, t, group, tile_rows - ITERS + i)

    def gather_columns(pieces, group):
        packed = {}
        for name_, _ in pieces:
            for side in range(2):
                packed[name_, side] = [jnp.zeros((SUB, LANES), jnp.float32) for _ in range(2)]
        for r in range(tile_rows):
            half, spot_ = divmod(r, SLOTS)
            here = block == spot_
            for name_, source in pieces:
                last = pltpu.roll(
                    planes_at(source, tiles - 1, group, r), (PACK * (spot_ + 1)) % LANES, 1
                )
                first = pltpu.roll(planes_at(source, 0, group, r), PACK * spot_, 1)
                packed[name_, 0][half] = jnp.where(here, last, packed[name_, 0][half])
                packed[name_, 1][half] = jnp.where(here, first, packed[name_, 1][half])
        return packed

    def put_columns(pieces, group, at):
        packed = gather_columns(pieces, group)
        count = len(pieces)
        for side, slab in enumerate((slab_e, slab_w)):
            for n, (name_, _) in enumerate(pieces):
                for half in range(2):
                    place = at + (2 * n + half) * SUB
                    slab[place : place + SUB, :] = packed[name_, side][half]
                    short = at // 2 + n * SUB
                    if half == 0:
                        corner_n[side, short : short + SUB, :] = packed[name_, side][half]
                    else:
                        corner_s[side, short : short + SUB, :] = packed[name_, side][half]

    sources = {
        NORTH: rows_n,
        SOUTH: rows_s,
        EAST: slab_e,
        WEST: slab_w,
        NE: corner_n.at[0],
        NW: corner_n.at[1],
        SE: corner_s.at[0],
        SW: corner_s.at[1],
    }
    sizes = {way: per if way < 2 else 4 * SUB if way < 4 else 2 * SUB for way in range(8)}

    def remote(way, group, arriving=False):
        sent = OPPOSITE[way] if arriving else way
        back = OPPOSITE[sent]
        size = sizes[way]
        if isinstance(group, int) and group == 0:
            place = pl.ds(0, 2 * size)
        else:
            place = pl.ds(pl.multiple_of((group + 1) * size, SUB), size)
        return pltpu.make_async_remote_copy(
            src_ref=sources[sent].at[place, :],
            dst_ref=received[back].at[place, :],
            send_sem=send_sem.at[group * 8 + sent],
            recv_sem=recv_sem.at[group * 8 + back],
            device_id=device(way),
            device_id_type=MESH,
        )

    for group in range(groups):
        for copy in loads[group]:
            copy.wait()
        if group == 0:
            put_columns((("x", along_x), ("y", along_y)), 0, 0)
        put_columns((("v", field), ("d", spread)), group, (group + 1) * 4 * SUB)
        if group == 0:
            greeted = jnp.int32(ncol - 1)
            for way in GREETED:
                greeted = greeted + exists(way).astype(jnp.int32)
            pl.semaphore_wait(barrier, greeted)
        for way in (EAST, WEST, NE, NW, SE, SW):

            @pl.when(exists(way))
            def _(way=way, group=group):
                remote(way, group).start()

        if group == 0:
            gather_rows(along_x, 0, 0)
            gather_rows(along_y, 0, ITERS * wide)
        gather_rows(field, group, (group + 1) * per)
        gather_rows(spread, group, (group + 1) * per + ITERS * wide)
        for way in (NORTH, SOUTH):

            @pl.when(exists(way))
            def _(way=way, group=group):
                remote(way, group).start()

    def own_strip(side, array, group, slab, base, group_base):
        halves = [
            slab[pl.ds(base + 2 * array * SUB + half * SUB, SUB), :] for half in range(2)
        ]
        t = tiles - 1 if side == 0 else 0
        begin = LANES - PACK if side == 0 else 0
        for got, first_slot in ((got_n, 2 * SLOTS - ITERS), (got_s, tile_rows)):
            for i in range(ITERS):
                spot_ = first_slot + i - SLOTS
                at = group_base + (array * ITERS + i) * wide + t * SUB
                moved = pltpu.roll(
                    got[pl.ds(at, SUB), :], (PACK * spot_ - begin) % LANES, 1
                )
                halves[1] = jnp.where(block == spot_, moved, halves[1])
        return halves

    def other_strip(side, array, got, base, corner_base):
        halves = [got[pl.ds(base + 2 * array * SUB + half * SUB, SUB), :] for half in range(2)]
        above = got_corner[side, pl.ds(corner_base + array * SUB, SUB), :]
        below = got_corner[2 + side, pl.ds(corner_base + array * SUB, SUB), :]
        first_above = 2 * SLOTS - ITERS - SLOTS
        first_below = tile_rows - SLOTS
        shift_above = (PACK * (first_above - (tile_rows - ITERS) % SLOTS)) % LANES
        shift_below = (PACK * first_below) % LANES
        halves[1] = jnp.where(block >= first_above, pltpu.roll(above, shift_above, 1), halves[1])
        halves[1] = jnp.where(
            jnp.logical_and(block >= first_below, block < first_below + ITERS),
            pltpu.roll(below, shift_below, 1),
            halves[1],
        )
        return halves

    def variants(value):
        sub = lax.broadcasted_iota(jnp.int32, (SUB, LANES), 0)
        out = []
        for group in range(groups):
            shift = (group * SUB) % levels
            if shift == 0:
                out.append(value)
            else:
                out.append(
                    jnp.where(
                        sub + shift < SUB,
                        pltpu.roll(value, SUB - shift, 0),
                        pltpu.roll(value, levels - shift, 0),
                    )
                )
        return out

    def wait_halo(group):
        for way in range(8):

            @pl.when(exists(way))
            def _(way=way):
                remote(way, group, True).wait_recv()

    def share_coefs():
        for which, got in enumerate((got_n, got_s)):

            def one(n, _, got=got, which=which):
                at = pl.multiple_of(n * SUB, SUB)
                for group, value in enumerate(variants(0.5 * got[pl.ds(at, SUB), :])):
                    halo_coef[group, which, pl.ds(at, SUB), :] = value
                return 0

            lax.fori_loop(0, per // SUB, one, 0, unroll=6)
        for side, (slab, got) in enumerate(((slab_e, got_e), (slab_w, got_w))):
            for array in range(2):
                own = own_strip(side, array, 0, slab, 0, 0)
                other = other_strip(side, array, got, 0, 0)
                for n, value in enumerate(own + other):
                    for group, moved in enumerate(variants(0.5 * value)):
                        at = (array * 4 + n) * SUB
                        edge_coef[group, side, at : at + SUB, :] = moved

    def products(v, d, hx, hy):
        p, x, y = d * v, hx * v, hy * v
        return v - 4.0 * p, p + x, p - x, p + y, p - y

    def swap(value):
        return jnp.concatenate([value[SUB:], value[:SUB]], 0)

    def next_rows(value):
        moved = pltpu.roll(value, PACK, 1)
        return jnp.where(lane_pair < PACK, swap(moved), moved)

    def previous_rows(value):
        moved = pltpu.roll(value, LANES - PACK, 1)
        return jnp.where(lane_pair >= LANES - PACK, swap(moved), moved)

    def strips(group):
        base = pl.multiple_of((group + 1) * 4 * SUB, SUB)
        corner_base = pl.multiple_of((group + 1) * 2 * SUB, SUB)
        group_base = pl.multiple_of((group + 1) * per, SUB)
        for side, (slab, got) in enumerate(((slab_e, got_e), (slab_w, got_w))):
            pairs = []
            for array in range(2):
                own = own_strip(side, array, group, slab, base, group_base)
                other = other_strip(side, array, got, base, corner_base)
                both = [jnp.concatenate(own, 0), jnp.concatenate(other, 0)]
                pairs.append(both if side == 0 else both[::-1])
            for array in range(2):
                at = array * 4 * SUB
                both = [
                    edge_coef[group, side, at : at + 2 * SUB, :],
                    edge_coef[group, side, at + 2 * SUB : at + 4 * SUB, :],
                ]
                pairs.append(both if side == 0 else both[::-1])
            now, d, hx, hy = pairs
            for sweep in range(ITERS):
                parts = [products(now[n], d[n], hx[n], hy[n]) for n in range(2)]
                edges[side, sweep] = parts[1][3] if side == 0 else parts[0][4]
                if sweep == ITERS - 1:
                    break
                right, left = [part[3] for part in parts], [part[4] for part in parts]
                rights = [
                    jnp.where(
                        inner == PACK - 1,
                        pltpu.roll(right[1], PACK - 1, 1),
                        pltpu.roll(right[0], LANES - 1, 1),
                    ),
                    pltpu.roll(right[1], LANES - 1, 1),
                ]
                lefts = [
                    pltpu.roll(left[0], 1, 1),
                    jnp.where(
                        inner == 0,
                        pltpu.roll(left[0], LANES - PACK + 1, 1),
                        pltpu.roll(left[1], 1, 1),
                    ),
                ]
                now = [
                    parts[n][0]
                    + previous_rows(parts[n][1])
                    + next_rows(parts[n][2])
                    + (rights[n] + lefts[n])
                    for n in range(2)
                ]

    def march(group):
        shift = lax.rem(group * SUB, levels)
        at_last, at_first = lane_wide == LANES - 1, lane_wide == 0

        def row_of(ref, r, which):
            return jnp.concatenate([planes_at(ref, t, which, r) for t in range(tiles)], 0)

        def coef_row(ref, r):
            start = shift * tile_rows + r
            return 0.5 * jnp.concatenate(
                [ref[t, pl.ds(start, SUB, stride=tile_rows), :] for t in range(tiles)], 0
            )

        def fetch(r):
            if isinstance(r, int) and not 0 <= r < tile_rows:
                which, i = (0, r + ITERS) if r < 0 else (1, r - tile_rows)
                got = (got_n, got_s)[which]
                base = pl.multiple_of((group + 1) * per, SUB)
                v = got[pl.ds(base + i * wide, wide), :]
                d = got[pl.ds(base + (ITERS + i) * wide, wide), :]
                hx = halo_coef[group, which, i * wide : (i + 1) * wide, :]
                hy = halo_coef[group, which, (ITERS + i) * wide : (ITERS + i + 1) * wide, :]
                return v, (d, hx, hy)
            return (
                row_of(field, r, group),
                (row_of(spread, r, group), coef_row(along_x, r), coef_row(along_y, r)),
            )

        def beyond(side, sweep, r):
            if isinstance(r, int):
                half, spot_ = divmod(r % (2 * SLOTS), SLOTS)
            else:
                half, spot_ = r // SLOTS, r % SLOTS
            value = edges[side, sweep, pl.ds(pl.multiple_of(half * SUB, SUB), SUB), :]
            if side == 0:
                amount = LANES - 1 - PACK * spot_
            else:
                amount = LANES - PACK + 1 - PACK * spot_
                amount = amount % LANES if isinstance(r, int) else amount
            return pltpu.roll(value, amount, 1)

        def lateral(right, left, sweep, r):
            right, left = pltpu.roll(right, LANES - 1, 1), pltpu.roll(left, 1, 1)
            from_right = jnp.concatenate([right[SUB:], beyond(0, sweep, r)], 0)
            from_left = jnp.concatenate([beyond(1, sweep, r), left[: wide - SUB]], 0)
            return jnp.where(at_last, from_right, right) + jnp.where(at_first, from_left, left)

        def finish_row(r, v):
            at = r * wide if isinstance(r, int) else pl.multiple_of(r * wide, SUB)
            out = keep[pl.ds(at, wide), :] * v
            for t in range(tiles):
                start = group * (SUB * tile_rows) + r
                nest[t, pl.ds(start, SUB, stride=tile_rows), :] = out[t * SUB : (t + 1) * SUB]
            return weigh[pl.ds(at, wide), :] * v

        def put_sum(g, value):
            at = g * SUB if isinstance(g, int) else pl.multiple_of(g * SUB, SUB)
            for t in range(tiles):
                sums[pl.ds(at, SUB), t * LANES : (t + 1) * LANES] = value[t * SUB : (t + 1) * SUB]

        def step(r, state):
            accs, downs, coefs = state
            accs, downs = list(accs), list(downs)
            v, coef = fetch(r)
            coefs = [coef] + list(coefs)
            static = isinstance(r, int)
            for sweep in range(ITERS):
                here = r - sweep
                first = static and here == sweep - ITERS
                last = static and here == tile_rows + ITERS - 1 - sweep
                d, hx, hy = coefs[sweep]
                if first:
                    downs[sweep] = (d - hx) * v
                    v = None
                    break
                if last:
                    v = accs[sweep] + (d + hx) * v
                    continue
                center, up, down, right, left = products(v, d, hx, hy)
                later = None if accs[sweep] is None else accs[sweep] + up
                accs[sweep] = center + lateral(right, left, sweep, here) + downs[sweep]
                downs[sweep] = down
                v = later
                if v is None:
                    break
            return (accs, downs, coefs[: ITERS - 1]), v

        state = ([None] * ITERS, [None] * ITERS, [])
        for r in range(-ITERS, ITERS):
            state, _ = step(r, state)

        def chunk(c, flat):
            state = jax.tree.unflatten(tree, flat)
            for i in range(CHUNK):
                r = ITERS + c * CHUNK + i
                state, v = step(r, state)
                term = finish_row(r - ITERS, v)
                total = term if i % 3 == 0 else total + term
                if i % 3 == 2:
                    put_sum(c * (CHUNK // 3) + i // 3, total)
            return tuple(jax.tree.leaves(state))

        flat, tree = jax.tree.flatten(state)
        chunks = (tile_rows - ITERS) // CHUNK
        flat = lax.fori_loop(0, chunks, chunk, tuple(flat))
        state = jax.tree.unflatten(tree, flat)
        total = None
        for r in range(ITERS + chunks * CHUNK, tile_rows + ITERS):
            state, v = step(r, state)
            term = finish_row(r - ITERS, v)
            total = term if (r - ITERS) % 3 == 0 else total + term
            if (r - ITERS) % 3 == 2:
                put_sum((r - ITERS) // 3, total)

    def to_owner(group, step):
        owner = lax.rem(col + step, ncol)
        rows = CAP * SUB
        return pltpu.make_async_remote_copy(
            src_ref=outbound.at[group, owner],
            dst_ref=arrived.at[group, pl.ds(step * rows, rows), :],
            send_sem=out_sem.at[group * ncol + step],
            recv_sem=in_sem.at[group * ncol + step],
            device_id=(row, owner),
            device_id_type=MESH,
        )

    tag_row = lax.broadcasted_iota(jnp.int32, (coarse_rows * SUB, LANES), 0) % SUB == 0

    def one_group(group, _):
        @pl.when(group > 0)
        def _():
            wait_halo(group)

        strips(group)
        march(group)
        high, low = split(sums[...])
        coarse = dot(high, pick[...]) + dot(low, pick[...])
        coarse = jnp.where(jnp.logical_and(tag_row, group == 0), tags[...], coarse)
        high, low = split(coarse)
        routed = dot(route[...], high) + dot(route[...], low)
        for k in range(ncol):
            outbound[group, k] = routed[k * CAP * SUB : (k + 1) * CAP * SUB]
        for step in range(1, ncol):
            to_owner(group, step).start()
        arrived[group, 0 : CAP * SUB, :] = outbound[group, col]
        return 0

    wait_halo(0)
    share_coefs()
    lax.fori_loop(0, groups, one_group, 0)

    for group in range(groups):
        for step in range(1, ncol):
            to_owner(group, step).wait_recv()
    for group in range(groups):
        for way in range(8):

            @pl.when(exists(way))
            def _(way=way, group=group):
                remote(way, group).wait_send()

    for group in range(groups):
        for step in range(1, ncol):
            to_owner(group, step).wait_send()


def finish(dims, nest, arrived, nest_hbm, parent_ref, store_sem):
    fields, levels, tile_rows, tiles, ncol = dims
    planes = fields * levels
    padded = round_up(planes + 1, SUB)
    lead = padded - planes
    stores = []
    for t in range(tiles):
        copy = pltpu.make_async_copy(
            nest.at[t, lead * tile_rows : padded * tile_rows, :],
            nest_hbm.at[:, t * LANES : (t + 1) * LANES],
            store_sem.at[t],
        )
        copy.start()
        stores.append(copy)

    count = ncol * CAP
    tags = arrived[0, pl.ds(0, count, stride=SUB), :]
    parent_row = lax.broadcasted_iota(jnp.int32, (count, LANES), 1).astype(jnp.float32) + 1.0
    picked = (tags == parent_row).astype(jnp.float32)
    stack = jnp.concatenate(
        [picked, picked, jnp.zeros((LANES - 2 * count, LANES), jnp.float32)], 0
    )
    picker = stack.T[:PROWS].astype(jnp.bfloat16)
    filler = jnp.zeros((LANES - 2 * count, LANES), jnp.bfloat16)
    for p in range(planes):
        group, sub = divmod(p + lead, SUB)
        value = arrived[group, pl.ds(sub, count, stride=SUB), :]
        high, low = split(value)
        parent_ref[p] = dot(picker, jnp.concatenate([high, low, filler], 0))
    for copy in stores:
        copy.wait()


def shards(adjoint_field, advect_x, advect_y, diffusion, zone_cells, feedback_dest, feedback_slot):
    fields, levels, tile_rows, tile_cols = adjoint_field.shape
    planes = fields * levels
    tiles = tile_cols // LANES
    ncol = lax.axis_size("col")
    padded = round_up(planes + 1, SUB)
    groups = padded // SUB
    runs = len(level_runs(levels, padded - planes))
    coarse_rows = tile_rows // 3
    wide = tiles * SUB
    f32 = jnp.float32
    vmem = pltpu.VMEM
    dma = pltpu.SemaphoreType.DMA
    smem_spec = pl.BlockSpec(memory_space=pltpu.SMEM)
    any_spec = pl.BlockSpec(memory_space=pl.ANY)
    vmem_spec = pl.BlockSpec(memory_space=pltpu.VMEM)
    own = (tiles, padded * tile_rows, LANES)
    level_own = (tiles, (levels + SUB - 1) * tile_rows, LANES)
    halo_rows = ((groups + 1) * 2 * ITERS * wide, LANES)
    halo_cols = ((groups + 1) * 4 * SUB, LANES)
    halo_corner = (groups + 1) * 2 * SUB
    nest, arrived = pl.pallas_call(
        functools.partial(kernel, (fields, levels, tile_rows, tiles)),
        out_shape=[
            pltpu.VMEM(own, f32),
            pltpu.VMEM((groups, ncol * CAP * SUB, LANES), f32),
        ],
        in_specs=[smem_spec] * 3 + [any_spec] * 4,
        out_specs=[vmem_spec] * 2,
        scratch_shapes=[
            vmem(own, f32),
            vmem(own, f32),
            vmem(level_own, f32),
            vmem(level_own, f32),
            vmem((tile_rows, LANES), f32),
            vmem((tile_rows * wide, LANES), f32),
            vmem((tile_rows * wide, LANES), f32),
            vmem((coarse_rows * SUB, tiles * LANES), f32),
            vmem((tiles * LANES, LANES), jnp.bfloat16),
            vmem((ncol * CAP * SUB, coarse_rows * SUB), jnp.bfloat16),
            vmem((coarse_rows * SUB, LANES), f32),
            vmem((groups, ncol, CAP * SUB, LANES), f32),
        ]
        + [vmem(halo_rows, f32)] * 4
        + [vmem(halo_cols, f32)] * 4
        + [
            vmem((2, halo_corner, LANES), f32),
            vmem((2, halo_corner, LANES), f32),
            vmem((4, halo_corner, LANES), f32),
            vmem((groups, 2, 2 * ITERS * wide, LANES), f32),
            vmem((groups, 2, 8 * SUB, LANES), f32),
            vmem((2, ITERS, 2 * SUB, LANES), f32),
            dma((2 * tiles * (groups + runs),)),
            dma((8 * groups,)),
            dma((8 * groups,)),
            dma((groups * ncol,)),
            dma((groups * ncol,)),
        ],
        compiler_params=pltpu.CompilerParams(
            collective_id=0, has_side_effects=True, vmem_limit_bytes=61 * 1024 * 1024
        ),
    )(
        zone_cells,
        feedback_dest.reshape(-1),
        feedback_slot.reshape(-1),
        adjoint_field.reshape(planes * tile_rows, tile_cols),
        diffusion.reshape(planes * tile_rows, tile_cols),
        advect_x.reshape(levels * tile_rows, tile_cols),
        advect_y.reshape(levels * tile_rows, tile_cols),
    )
    nest, parent = pl.pallas_call(
        functools.partial(finish, (fields, levels, tile_rows, tiles, ncol)),
        out_shape=(
            jax.ShapeDtypeStruct((planes * tile_rows, tile_cols), f32),
            jax.ShapeDtypeStruct((planes, PROWS, LANES), f32),
        ),
        in_specs=[vmem_spec] * 2,
        out_specs=(any_spec, vmem_spec),
        scratch_shapes=[dma((tiles,))],
        compiler_params=pltpu.CompilerParams(vmem_limit_bytes=16 * 1024 * 1024),
    )(nest, arrived)
    return (
        nest.reshape(adjoint_field.shape),
        parent.reshape(fields, levels, PROWS, LANES),
    )


def solution(mesh):
    placed = (
        P(None, None, "row", "col"),
        P(None, "row", "col"),
        P(None, "row", "col"),
        P(None, None, "row", "col"),
        P(),
        P("col", "row", None),
        P("col", "row", None),
    )
    return jax.shard_map(
        shards,
        mesh=mesh,
        in_specs=placed,
        out_specs=(P(None, None, "row", "col"), P(None, None, "row", "col")),
        check_vma=False,
    )
```

```python
import functools
import math

import jax
import jax.numpy as jnp
from jax import lax
from jax.experimental import pallas as pl
from jax.experimental.pallas import tpu as pltpu
from jax.sharding import PartitionSpec as P

ITERS = 3
PROWS = 80
CAP = 2
LANES = 128
SUB = 8
PACK = 4
PAIR = 2 * PACK
SLOTS = LANES // PAIR
CHUNK = 45
MESH = pl.DeviceIdType.MESH
DIRS = ((-1, 0), (1, 0), (0, 1), (0, -1), (-1, 1), (-1, -1), (1, 1), (1, -1))
NORTH, SOUTH, EAST, WEST, NE, NW, SE, SW = range(8)
OPPOSITE = (SOUTH, NORTH, WEST, EAST, SW, SE, NW, NE)
GREETED = (NORTH, SOUTH, NE, NW, SE, SW)


def round_up(value, step):
    return -(-value // step) * step


def split(values):
    high = values.astype(jnp.bfloat16)
    return high, (values - high.astype(jnp.float32)).astype(jnp.bfloat16)


def dot(left, right):
    return jnp.dot(left, right, preferred_element_type=jnp.float32)


def variants_of(groups, levels):
    return min(groups, levels // math.gcd(levels, SUB))


def kernel(
    dims,
    zone_ref,
    dest_ref,
    slot_ref,
    field_hbm,
    spread_hbm,
    along_x_hbm,
    along_y_hbm,
    nest,
    parent,
    arrived,
    field,
    spread,
    along_x,
    along_y,
    ramps,
    keep,
    weigh,
    sums,
    pick,
    route,
    tags,
    outbound,
    rows_n,
    rows_s,
    got_n,
    got_s,
    slab,
    got_e,
    got_w,
    got_corner,
    halo_coef,
    edge_coef,
    edges,
    load_sem,
    send_sem,
    recv_sem,
    out_sem,
    in_sem,
):
    fields, levels, tile_rows, tiles = dims
    planes = fields * levels
    padded = round_up(planes + 1, SUB)
    groups, lead = padded // SUB, padded - planes
    wide = tiles * SUB
    per = 2 * ITERS * wide
    row, col = lax.axis_index("row"), lax.axis_index("col")
    nrow, ncol = lax.axis_size("row"), lax.axis_size("col")
    coarse_rows = tile_rows // 3

    def exists(way):
        down, over = DIRS[way]
        conditions = []
        if down < 0:
            conditions.append(row > 0)
        if down > 0:
            conditions.append(row < nrow - 1)
        if over < 0:
            conditions.append(col > 0)
        if over > 0:
            conditions.append(col < ncol - 1)
        return functools.reduce(jnp.logical_and, conditions)

    def device(way):
        return (row + DIRS[way][0], col + DIRS[way][1])

    def aligned(value):
        return value if isinstance(value, int) else pl.multiple_of(value, SUB)

    orders = variants_of(groups, levels)
    thirds = tile_rows // SLOTS
    strip = thirds * 2 * SUB
    arrays = ((field_hbm, field), (spread_hbm, spread), (along_x_hbm, along_x), (along_y_hbm, along_y))

    def load_group(group):
        for place in range(group * SUB, (group + 1) * SUB):
            for n, (source, target) in enumerate(arrays):
                if n < 2 and place < lead or n >= 2 and group >= orders:
                    continue
                number = place - lead if n < 2 else (place - lead) % levels
                pltpu.make_async_copy(
                    source.at[number * tile_rows : (number + 1) * tile_rows, :],
                    target.at[:, place, :],
                    load_sem.at[group * len(arrays) + n],
                ).start()

    def wait_loads(group):
        for n, (_, target) in enumerate(arrays):
            if n >= 2 and group >= orders:
                continue
            first = max(group * SUB, lead) if n < 2 else group * SUB
            region = target.at[:, first : (group + 1) * SUB, :]
            pltpu.make_async_copy(region, region, load_sem.at[group * len(arrays) + n]).wait()

    load_group(0)

    barrier = pltpu.get_barrier_semaphore()
    for way in GREETED:

        @pl.when(exists(way))
        def _(way=way):
            pl.semaphore_signal(barrier, inc=1, device_id=device(way), device_id_type=MESH)

    for step in range(1, ncol):
        pl.semaphore_signal(
            barrier, inc=1, device_id=(row, lax.rem(col + step, ncol)), device_id_type=MESH
        )

    lane = lax.broadcasted_iota(jnp.int32, (SUB, LANES), 1)
    block = lane // PAIR
    lane_wide = lax.broadcasted_iota(jnp.int32, (wide, LANES), 1)
    lane_strip = lax.broadcasted_iota(jnp.int32, ((thirds + 1) * SUB, LANES), 1)
    inner = lane_strip % PAIR

    for ref in (field, spread):
        ref[:, 0:lead, :] = jnp.zeros((tile_rows, lead, tiles * LANES), jnp.float32)

    received = {NORTH: got_n, SOUTH: got_s, EAST: got_e, WEST: got_w}
    for place, way in enumerate((NE, NW, SE, SW)):
        received[way] = got_corner.at[place]
    for way in range(8):

        @pl.when(jnp.logical_not(exists(way)))
        def _(way=way):
            received[way][...] = jnp.zeros(received[way].shape, jnp.float32)

    def planes_at(ref, t, group, r):
        at = group * SUB if isinstance(group, int) else pl.multiple_of(group * SUB, SUB)
        return ref[r, pl.ds(at, SUB), t * LANES : (t + 1) * LANES]

    def both_edges(first, last, spot_):
        return pltpu.roll(jnp.where(lane < PACK, first, last), PAIR * spot_ + PACK, 1)

    def gather_rows(source, group, at):
        for i in range(ITERS):
            for t in range(tiles):
                place = slice(at + i * wide + t * SUB, at + i * wide + (t + 1) * SUB)
                rows_n[place, :] = planes_at(source, t, group, i)
                rows_s[place, :] = planes_at(source, t, group, tile_rows - ITERS + i)

    def put_columns(pieces, group, at):
        for n, source in enumerate(pieces):
            for third in range(thirds):
                value = jnp.zeros((SUB, LANES), jnp.float32)
                for spot_ in range(SLOTS):
                    r = third * SLOTS + spot_
                    moved = both_edges(
                        planes_at(source, 0, group, r),
                        planes_at(source, tiles - 1, group, r),
                        spot_,
                    )
                    value = jnp.where(block == spot_, moved, value)
                place = at + (2 * third + n) * SUB
                slab[place : place + SUB, :] = value

    def fill_tables():
        def ramp(position, count, low_zone, high_zone):
            shape = position.shape
            scale_low = jnp.full(shape, (low_zone + 1).astype(jnp.float32))
            scale_high = jnp.full(shape, (high_zone + 1).astype(jnp.float32))
            lower = jnp.maximum(low_zone - position, 0).astype(jnp.float32) / scale_low
            upper = jnp.maximum(high_zone - (count - 1 - position), 0).astype(jnp.float32) / scale_high
            return jnp.maximum(lower, upper)

        row_index = row * tile_rows + lax.broadcasted_iota(jnp.int32, (tile_rows, LANES), 0)
        ramps[...] = ramp(row_index, tile_rows * nrow, zone_ref[0], zone_ref[1])
        tile_index = lax.broadcasted_iota(jnp.int32, (wide, LANES), 0) // SUB
        weight_cols = ramp(
            (col * tiles + tile_index) * LANES + lane_wide,
            tiles * LANES * ncol,
            zone_ref[2],
            zone_ref[3],
        )

        def weights(r, _):
            across = jnp.broadcast_to(ramps[pl.ds(r, 1), :], (wide, LANES))
            relaxation = jnp.maximum(across, weight_cols)
            at = pl.multiple_of(r * wide, SUB)
            keep[pl.ds(at, wide), :] = 1.0 - relaxation
            weigh[pl.ds(at, wide), :] = (1.0 - relaxation) / 9.0 + relaxation
            return 0

        lax.fori_loop(0, tile_rows, weights, 0, unroll=4)

        fine = lax.broadcasted_iota(jnp.int32, (tiles * LANES, LANES), 0)
        name = lax.broadcasted_iota(jnp.int32, (tiles * LANES, LANES), 1)
        pick[...] = (fine // 3 == name).astype(jnp.float32).astype(jnp.bfloat16)

        dests = [dest_ref[g] for g in range(coarse_rows)]
        from_lane = lax.broadcasted_iota(jnp.int32, (SUB, coarse_rows * SUB), 1)
        spot = jnp.zeros((SUB, coarse_rows * SUB), jnp.int32)
        for g in range(coarse_rows):
            rank = jnp.int32(0)
            for before in range(g):
                rank = rank + jnp.where(dests[before] == dests[g], 1, 0)
            spot = jnp.where(from_lane // SUB == g, dests[g] * CAP + rank, spot)
            tags[g * SUB : (g + 1) * SUB, :] = jnp.full(
                (SUB, LANES), (slot_ref[g] + 1).astype(jnp.float32)
            )
        same = from_lane % SUB == lax.broadcasted_iota(jnp.int32, (SUB, coarse_rows * SUB), 0)
        spot = jnp.where(same, spot, -1)
        for k in range(0, ncol * CAP, 2):
            pair = jnp.concatenate(
                [(spot == k).astype(jnp.float32), (spot == k + 1).astype(jnp.float32)], 0
            )
            route[k * SUB : (k + 2) * SUB, :] = pair.astype(jnp.bfloat16)

    sources = {NORTH: rows_n, SOUTH: rows_s}

    def remote(way, group, arriving=False, coefs=False):
        sent = OPPOSITE[way] if arriving else way
        back = OPPOSITE[sent]
        whole = per if sent < 2 else strip
        if sent >= 4:
            third = 0 if sent in (NE, NW) else thirds - 1
            count = 2 * SUB
            part = 0 if coefs else group + 1
            source = slab.at[pl.ds(aligned(part * strip + third * count), count), :]
            target = received[back].at[pl.ds(aligned(part * count), count), :]
        else:
            if isinstance(group, int) and group == 0:
                place = pl.ds(0, 2 * whole)
            else:
                place = pl.ds(aligned((group + 1) * whole), whole)
            source = sources.get(sent, slab).at[place, :]
            target = received[back].at[place, :]
        return pltpu.make_async_remote_copy(
            src_ref=source,
            dst_ref=target,
            send_sem=send_sem.at[sent],
            recv_sem=recv_sem.at[group * 8 + back],
            device_id=device(way),
            device_id_type=MESH,
        )

    def each(way, group, arriving=False):
        copies = [remote(way, group, arriving)]
        if way >= 4 and isinstance(group, int) and group == 0:
            copies.append(remote(way, group, arriving, True))
        return copies

    for group in range(groups):
        if group == 1:
            fill_tables()
        wait_loads(group)
        if group == 0:
            put_columns((along_x, along_y), 0, 0)
        put_columns((field, spread), group, (group + 1) * strip)
        if group == 0:
            greeted = jnp.int32(ncol - 1)
            for way in GREETED:
                greeted = greeted + exists(way).astype(jnp.int32)
            pl.semaphore_wait(barrier, greeted)
        for way in (EAST, WEST, NE, NW, SE, SW):

            @pl.when(exists(way))
            def _(way=way, group=group):
                for copy in each(way, group):
                    copy.start()

        if group == 0:
            gather_rows(along_x, 0, 0)
            gather_rows(along_y, 0, ITERS * wide)
        gather_rows(field, group, (group + 1) * per)
        gather_rows(spread, group, (group + 1) * per + ITERS * wide)
        for way in (NORTH, SOUTH):

            @pl.when(exists(way))
            def _(way=way, group=group):
                for copy in each(way, group):
                    copy.start()

        if group == 0:
            for later in range(1, groups):
                load_group(later)

    def strip_of(array, base, corner_base, group_base):
        halo = jnp.zeros((SUB, LANES), jnp.float32)
        for got, first_slot in ((got_n, SLOTS - ITERS), (got_s, 0)):
            for i in range(ITERS):
                at = group_base + (array * ITERS + i) * wide
                moved = both_edges(
                    got[pl.ds(at, SUB), :],
                    got[pl.ds(at + (tiles - 1) * SUB, SUB), :],
                    first_slot + i,
                )
                halo = jnp.where(block == first_slot + i, moved, halo)

        def whole(ref, last):
            parts = [
                ref[pl.ds(base + (2 * third + array) * SUB, SUB), :] for third in range(thirds)
            ]
            return jnp.concatenate(parts + [last], 0)

        own = whole(slab, halo)
        out = []
        for side, got in enumerate((got_e, got_w)):
            corner = pl.ds(corner_base + array * SUB, SUB)
            last = jnp.where(
                block >= SLOTS - ITERS, got_corner[side, corner, :], got_corner[2 + side, corner, :]
            )
            last = jnp.where(
                jnp.logical_or(block >= SLOTS - ITERS, block < ITERS), last, jnp.zeros_like(last)
            )
            other = whole(got, last)
            west, east = (own, other) if side == 0 else (other, own)
            out.append(jnp.where(inner < PACK, west, east))
        return out

    def variants(value):
        sub = lax.broadcasted_iota(jnp.int32, (SUB, LANES), 0)
        out = []
        for group in range(groups):
            shift = (group * SUB) % levels
            if shift == 0:
                out.append(value)
            else:
                out.append(
                    jnp.where(
                        sub + shift < SUB,
                        pltpu.roll(value, SUB - shift, 0),
                        pltpu.roll(value, levels - shift, 0),
                    )
                )
        return out

    def wait_halo(group):
        for way in range(8):

            @pl.when(exists(way))
            def _(way=way):
                if way >= 4 and isinstance(group, int) and group == 0:
                    region = received[way].at[0 : 4 * SUB, :]
                    pltpu.make_async_copy(region, region, recv_sem.at[way]).wait()
                else:
                    remote(way, group, True).wait_recv()

    def share_coefs():
        for which, got in enumerate((got_n, got_s)):

            def one(n, _, got=got, which=which):
                at = pl.multiple_of(n * SUB, SUB)
                for group, value in enumerate(variants(0.5 * got[pl.ds(at, SUB), :])):
                    halo_coef[group, which, pl.ds(at, SUB), :] = value
                return 0

            lax.fori_loop(0, per // SUB, one, 0, unroll=6)
        for array in range(2):
            for side, value in enumerate(strip_of(array, 0, 0, 0)):
                for third in range(thirds + 1):
                    at = (array * (thirds + 1) + third) * SUB
                    part = 0.5 * value[third * SUB : (third + 1) * SUB]
                    for group, moved in enumerate(variants(part)):
                        edge_coef[group, side, at : at + SUB, :] = moved

    def products(v, d, hx, hy):
        p, x, y = d * v, hx * v, hy * v
        return v - 4.0 * p, p + x, p - x, p + y, p - y

    def next_rows(value):
        moved = pltpu.roll(value, PAIR, 1)
        carried = jnp.concatenate([moved[thirds * SUB :], moved[: thirds * SUB]], 0)
        return jnp.where(lane_strip < PAIR, carried, moved)

    def previous_rows(value):
        moved = pltpu.roll(value, LANES - PAIR, 1)
        carried = jnp.concatenate([moved[SUB:], moved[:SUB]], 0)
        return jnp.where(lane_strip >= LANES - PAIR, carried, moved)

    def strips(group):
        base = pl.multiple_of((group + 1) * strip, SUB)
        corner_base = pl.multiple_of((group + 1) * 2 * SUB, SUB)
        group_base = pl.multiple_of((group + 1) * per, SUB)
        fields_now = strip_of(0, base, corner_base, group_base)
        spreads = strip_of(1, base, corner_base, group_base)
        count = (thirds + 1) * SUB
        flux = []
        for side in range(2):
            now, d = fields_now[side], spreads[side]
            hx = edge_coef[group, side, 0:count, :]
            hy = edge_coef[group, side, count : 2 * count, :]
            flux.append([])
            for sweep in range(ITERS):
                center, up, down, right, left = products(now, d, hx, hy)
                flux[side].append(right if side == 0 else left)
                if sweep < ITERS - 1:
                    now = (
                        center
                        + previous_rows(up)
                        + next_rows(down)
                        + (pltpu.roll(right, LANES - 1, 1) + pltpu.roll(left, 1, 1))
                    )
        for sweep in range(ITERS):
            edges[sweep] = jnp.where(
                inner == PACK, flux[0][sweep], pltpu.roll(flux[1][sweep], 2, 1)
            )

    def march(group):
        order = lax.rem(group, orders)
        at_last, at_first = lane_wide == LANES - 1, lane_wide == 0

        def row_of(ref, r, which):
            return jnp.concatenate([planes_at(ref, t, which, r) for t in range(tiles)], 0)

        def coef_row(ref, r):
            return 0.5 * row_of(ref, r, order)

        def fetch(r):
            if isinstance(r, int) and not 0 <= r < tile_rows:
                which, i = (0, r + ITERS) if r < 0 else (1, r - tile_rows)
                got = (got_n, got_s)[which]
                base = pl.multiple_of((group + 1) * per, SUB)
                v = got[pl.ds(base + i * wide, wide), :]
                d = got[pl.ds(base + (ITERS + i) * wide, wide), :]
                hx = halo_coef[group, which, i * wide : (i + 1) * wide, :]
                hy = halo_coef[group, which, (ITERS + i) * wide : (ITERS + i + 1) * wide, :]
                return v, (d, hx, hy)
            return (
                row_of(field, r, group),
                (row_of(spread, r, group), coef_row(along_x, r), coef_row(along_y, r)),
            )

        def lateral(right, left, sweep, r):
            if isinstance(r, int):
                part, spot_ = divmod(r % ((thirds + 1) * SLOTS), SLOTS)
            else:
                part, spot_ = r // SLOTS, r % SLOTS
            beyond = pltpu.roll(
                edges[sweep, pl.ds(aligned(part * SUB), SUB), :],
                LANES - 1 - PACK - PAIR * spot_,
                1,
            )
            right, left = pltpu.roll(right, LANES - 1, 1), pltpu.roll(left, 1, 1)
            from_right = jnp.concatenate([right[SUB:], beyond], 0)
            from_left = jnp.concatenate([beyond, left[: wide - SUB]], 0)
            return jnp.where(at_last, from_right, right) + jnp.where(at_first, from_left, left)

        def finish_row(r, v):
            at = r * wide if isinstance(r, int) else pl.multiple_of(r * wide, SUB)
            out = keep[pl.ds(at, wide), :] * v
            for t in range(tiles):
                place = pl.ds(pl.multiple_of(group * SUB, SUB), SUB)
                nest[r, place, t * LANES : (t + 1) * LANES] = out[t * SUB : (t + 1) * SUB]
            return weigh[pl.ds(at, wide), :] * v

        def put_sum(g, value):
            at = g * SUB if isinstance(g, int) else pl.multiple_of(g * SUB, SUB)
            for t in range(tiles):
                sums[pl.ds(at, SUB), t * LANES : (t + 1) * LANES] = value[t * SUB : (t + 1) * SUB]

        def step(r, state):
            accs, downs, coefs = state
            accs, downs = list(accs), list(downs)
            v, coef = fetch(r)
            coefs = [coef] + list(coefs)
            static = isinstance(r, int)
            for sweep in range(ITERS):
                here = r - sweep
                first = static and here == sweep - ITERS
                last = static and here == tile_rows + ITERS - 1 - sweep
                d, hx, hy = coefs[sweep]
                if first:
                    downs[sweep] = (d - hx) * v
                    v = None
                    break
                if last:
                    v = accs[sweep] + (d + hx) * v
                    continue
                center, up, down, right, left = products(v, d, hx, hy)
                later = None if accs[sweep] is None else accs[sweep] + up
                accs[sweep] = center + lateral(right, left, sweep, here) + downs[sweep]
                downs[sweep] = down
                v = later
                if v is None:
                    break
            return (accs, downs, coefs[: ITERS - 1]), v

        state = ([None] * ITERS, [None] * ITERS, [])
        for r in range(-ITERS, ITERS):
            state, _ = step(r, state)

        def chunk(c, flat):
            state = jax.tree.unflatten(tree, flat)
            for i in range(CHUNK):
                r = ITERS + c * CHUNK + i
                state, v = step(r, state)
                term = finish_row(r - ITERS, v)
                total = term if i % 3 == 0 else total + term
                if i % 3 == 2:
                    put_sum(c * (CHUNK // 3) + i // 3, total)
            return tuple(jax.tree.leaves(state))

        flat, tree = jax.tree.flatten(state)
        chunks = (tile_rows - ITERS) // CHUNK
        if chunks == 1:
            flat = chunk(0, flat)
        else:
            flat = lax.fori_loop(0, chunks, chunk, tuple(flat))
        state = jax.tree.unflatten(tree, flat)
        total = None
        for r in range(ITERS + chunks * CHUNK, tile_rows + ITERS):
            state, v = step(r, state)
            term = finish_row(r - ITERS, v)
            total = term if (r - ITERS) % 3 == 0 else total + term
            if (r - ITERS) % 3 == 2:
                put_sum((r - ITERS) // 3, total)

    def to_owner(group, step):
        owner = lax.rem(col + step, ncol)
        rows = CAP * SUB
        return pltpu.make_async_remote_copy(
            src_ref=outbound.at[group, owner],
            dst_ref=arrived.at[group, pl.ds(step * rows, rows), :],
            send_sem=out_sem.at[0],
            recv_sem=in_sem.at[group],
            device_id=(row, owner),
            device_id_type=MESH,
        )

    tag_row = lax.broadcasted_iota(jnp.int32, (coarse_rows * SUB, LANES), 0) % SUB == 0

    def one_group(group, _):
        @pl.when(group > 0)
        def _():
            wait_halo(group)

        strips(group)
        march(group)
        high, low = split(sums[...])
        coarse = dot(high, pick[...]) + dot(low, pick[...])
        coarse = jnp.where(jnp.logical_and(tag_row, group == 0), tags[...], coarse)
        high, low = split(coarse)
        routed = dot(route[...], high) + dot(route[...], low)
        for k in range(ncol):
            outbound[group, k] = routed[k * CAP * SUB : (k + 1) * CAP * SUB]
        for step in range(1, ncol):
            to_owner(group, step).start()
        arrived[group, 0 : CAP * SUB, :] = outbound[group, col]
        return 0

    wait_halo(0)
    share_coefs()
    lax.fori_loop(0, groups, one_group, 0)

    for way in range(8):

        @pl.when(exists(way))
        def _(way=way):
            pltpu.make_async_copy(received[way], received[way], send_sem.at[way]).wait()

    sent_away = outbound.at[:, 1:ncol]
    pltpu.make_async_copy(sent_away, sent_away, out_sem.at[0]).wait()

    count = ncol * CAP
    filler = jnp.zeros((LANES - 2 * count, LANES), jnp.bfloat16)
    for group in range(groups):
        region = arrived.at[group, CAP * SUB : ncol * CAP * SUB, :]
        pltpu.make_async_copy(region, region, in_sem.at[group]).wait()
        if group == 0:
            named = arrived[0, pl.ds(0, count, stride=SUB), :]
            lines = lax.broadcasted_iota(jnp.int32, (count, LANES), 1).astype(jnp.float32) + 1.0
            picked = (named == lines).astype(jnp.float32)
            stack = jnp.concatenate(
                [picked, picked, jnp.zeros((LANES - 2 * count, LANES), jnp.float32)], 0
            )
            picker = stack.T[:PROWS].astype(jnp.bfloat16)
        for place in range(group * SUB, (group + 1) * SUB):
            if place >= lead:
                high, low = split(arrived[group, pl.ds(place % SUB, count, stride=SUB), :])
                parent[place - lead] = dot(picker, jnp.concatenate([high, low, filler], 0))


def finish(dims, nest, parent, nest_hbm, parent_hbm, store_sem):
    fields, levels, tile_rows = dims
    planes = fields * levels
    lead = round_up(planes + 1, SUB) - planes
    whole = pltpu.make_async_copy(parent, parent_hbm, store_sem.at[1])
    whole.start()
    for p in range(planes):
        pltpu.make_async_copy(
            nest.at[:, lead + p, :],
            nest_hbm.at[p * tile_rows : (p + 1) * tile_rows, :],
            store_sem.at[0],
        ).start()
    pltpu.make_async_copy(nest_hbm, nest_hbm, store_sem.at[0]).wait()
    whole.wait()


def shards(adjoint_field, advect_x, advect_y, diffusion, zone_cells, feedback_dest, feedback_slot):
    fields, levels, tile_rows, tile_cols = adjoint_field.shape
    planes = fields * levels
    tiles = tile_cols // LANES
    ncol = lax.axis_size("col")
    padded = round_up(planes + 1, SUB)
    groups = padded // SUB
    orders = variants_of(groups, levels)
    thirds = tile_rows * PAIR // LANES
    coarse_rows = tile_rows // 3
    wide = tiles * SUB
    f32 = jnp.float32
    vmem = pltpu.VMEM
    dma = pltpu.SemaphoreType.DMA
    smem_spec = pl.BlockSpec(memory_space=pltpu.SMEM)
    any_spec = pl.BlockSpec(memory_space=pl.ANY)
    vmem_spec = pl.BlockSpec(memory_space=pltpu.VMEM)
    own = (tile_rows, padded, tile_cols)
    level_own = (tile_rows, orders * SUB, tile_cols)
    halo_rows = ((groups + 1) * 2 * ITERS * wide, LANES)
    halo_cols = ((groups + 1) * thirds * 2 * SUB, LANES)
    halo_corner = (groups + 1) * 2 * SUB
    nest, parent = pl.pallas_call(
        functools.partial(kernel, (fields, levels, tile_rows, tiles)),
        out_shape=[
            pltpu.VMEM(own, f32),
            pltpu.VMEM((planes, PROWS, LANES), f32),
        ],
        in_specs=[smem_spec] * 3 + [any_spec] * 4,
        out_specs=[vmem_spec] * 2,
        scratch_shapes=[
            vmem((groups, ncol * CAP * SUB, LANES), f32),
            vmem(own, f32),
            vmem(own, f32),
            vmem(level_own, f32),
            vmem(level_own, f32),
            vmem((tile_rows, LANES), f32),
            vmem((tile_rows * wide, LANES), f32),
            vmem((tile_rows * wide, LANES), f32),
            vmem((coarse_rows * SUB, tiles * LANES), f32),
            vmem((tiles * LANES, LANES), jnp.bfloat16),
            vmem((ncol * CAP * SUB, coarse_rows * SUB), jnp.bfloat16),
            vmem((coarse_rows * SUB, LANES), f32),
            vmem((groups, ncol, CAP * SUB, LANES), f32),
        ]
        + [vmem(halo_rows, f32)] * 4
        + [vmem(halo_cols, f32)] * 3
        + [
            vmem((4, halo_corner, LANES), f32),
            vmem((groups, 2, 2 * ITERS * wide, LANES), f32),
            vmem((groups, 2, 2 * (thirds + 1) * SUB, LANES), f32),
            vmem((ITERS, (thirds + 1) * SUB, LANES), f32),
            dma((4 * groups,)),
            dma((8,)),
            dma((8 * groups,)),
            dma((1,)),
            dma((groups,)),
        ],
        compiler_params=pltpu.CompilerParams(
            collective_id=0, has_side_effects=True, vmem_limit_bytes=60 * 1024 * 1024
        ),
    )(
        zone_cells,
        feedback_dest.reshape(-1),
        feedback_slot.reshape(-1),
        adjoint_field.reshape(planes * tile_rows, tile_cols),
        diffusion.reshape(planes * tile_rows, tile_cols),
        advect_x.reshape(levels * tile_rows, tile_cols),
        advect_y.reshape(levels * tile_rows, tile_cols),
    )
    nest, parent = pl.pallas_call(
        functools.partial(finish, (fields, levels, tile_rows)),
        out_shape=(
            jax.ShapeDtypeStruct((planes * tile_rows, tile_cols), f32),
            jax.ShapeDtypeStruct((planes, PROWS, LANES), f32),
        ),
        in_specs=[vmem_spec] * 2,
        out_specs=(any_spec, any_spec),
        scratch_shapes=[dma((2,))],
        compiler_params=pltpu.CompilerParams(vmem_limit_bytes=16 * 1024 * 1024),
    )(nest, parent)
    return (
        nest.reshape(adjoint_field.shape),
        parent.reshape(fields, levels, PROWS, LANES),
    )


def solution(mesh):
    placed = (
        P(None, None, "row", "col"),
        P(None, "row", "col"),
        P(None, "row", "col"),
        P(None, None, "row", "col"),
        P(),
        P("col", "row", None),
        P("col", "row", None),
    )
    return jax.shard_map(
        shards,
        mesh=mesh,
        in_specs=placed,
        out_specs=(P(None, None, "row", "col"), P(None, None, "row", "col")),
        check_vma=False,
    )
```

```python
import functools
import math

import jax
import jax.numpy as jnp
from jax import lax
from jax.experimental import pallas as pl
from jax.experimental.pallas import tpu as pltpu
from jax.sharding import PartitionSpec as P

ITERS = 3
PROWS = 80
CAP = 2
LANES = 128
SUB = 8
PACK = 4
PAIR = 2 * PACK
AHEAD = 2
SLOTS = LANES // PAIR
MESH = pl.DeviceIdType.MESH
DIRS = ((-1, 0), (1, 0), (0, 1), (0, -1), (-1, 1), (-1, -1), (1, 1), (1, -1))
NORTH, SOUTH, EAST, WEST, NE, NW, SE, SW = range(8)
OPPOSITE = (SOUTH, NORTH, WEST, EAST, SW, SE, NW, NE)
GREETED = (NORTH, SOUTH, NE, NW, SE, SW)


def round_up(value, step):
    return -(-value // step) * step


def split(values):
    high = values.astype(jnp.bfloat16)
    return high, (values - high.astype(jnp.float32)).astype(jnp.bfloat16)


def dot(left, right):
    return jnp.dot(left, right, preferred_element_type=jnp.float32)


def variants_of(groups, levels):
    return min(groups, levels // math.gcd(levels, SUB))


def kernel(
    dims,
    zone_ref,
    dest_ref,
    slot_ref,
    field_hbm,
    spread_hbm,
    along_x_hbm,
    along_y_hbm,
    nest,
    parent,
    arrived,
    field,
    spread,
    along_x,
    along_y,
    ramps,
    keep,
    weigh,
    sums,
    pick,
    route,
    tags,
    outbound,
    rows_n,
    rows_s,
    got_n,
    got_s,
    slab,
    got_e,
    got_w,
    got_corner,
    halo_coef,
    edge_coef,
    edges,
    between,
    load_sem,
    send_sem,
    recv_sem,
    out_sem,
    in_sem,
):
    fields, levels, tile_rows, tiles = dims
    planes = fields * levels
    padded = round_up(planes + 1, SUB)
    groups, lead = padded // SUB, padded - planes
    wide = tiles * SUB
    per = 2 * ITERS * wide
    row, col = lax.axis_index("row"), lax.axis_index("col")
    nrow, ncol = lax.axis_size("row"), lax.axis_size("col")
    coarse_rows = tile_rows // 3

    def exists(way):
        down, over = DIRS[way]
        conditions = []
        if down < 0:
            conditions.append(row > 0)
        if down > 0:
            conditions.append(row < nrow - 1)
        if over < 0:
            conditions.append(col > 0)
        if over > 0:
            conditions.append(col < ncol - 1)
        return functools.reduce(jnp.logical_and, conditions)

    def device(way):
        return (row + DIRS[way][0], col + DIRS[way][1])

    def aligned(value):
        return value if isinstance(value, int) else pl.multiple_of(value, SUB)

    orders = variants_of(groups, levels)
    thirds = tile_rows // SLOTS
    strip = thirds * 2 * SUB
    arrays = ((field_hbm, field), (spread_hbm, spread), (along_x_hbm, along_x), (along_y_hbm, along_y))

    def load_group(group):
        for place in range(group * SUB, (group + 1) * SUB):
            for n, (source, target) in enumerate(arrays):
                if n < 2 and place < lead or n >= 2 and group >= orders:
                    continue
                number = place - lead if n < 2 else (place - lead) % levels
                pltpu.make_async_copy(
                    source.at[number * tile_rows : (number + 1) * tile_rows, :],
                    target.at[:, place, :],
                    load_sem.at[group * len(arrays) + n],
                ).start()

    def wait_load(group, n):
        target = arrays[n][1]
        if isinstance(group, int):
            first = max(group * SUB, lead) if n < 2 else group * SUB
            region = target.at[:, first : (group + 1) * SUB, :]
        else:
            region = target.at[:, pl.ds(aligned(group * SUB), SUB), :]
        pltpu.make_async_copy(region, region, load_sem.at[group * len(arrays) + n]).wait()

    load_group(0)

    barrier = pltpu.get_barrier_semaphore()
    for way in GREETED:

        @pl.when(exists(way))
        def _(way=way):
            pl.semaphore_signal(barrier, inc=1, device_id=device(way), device_id_type=MESH)

    for step in range(1, ncol):
        pl.semaphore_signal(
            barrier, inc=1, device_id=(row, lax.rem(col + step, ncol)), device_id_type=MESH
        )

    lane = lax.broadcasted_iota(jnp.int32, (SUB, LANES), 1)
    block = lane // PAIR
    lane_wide = lax.broadcasted_iota(jnp.int32, (wide, LANES), 1)
    lane_strip = lax.broadcasted_iota(jnp.int32, ((thirds + 1) * SUB, LANES), 1)
    inner = lane_strip % PAIR

    for ref in (field, spread):
        ref[:, 0:lead, :] = jnp.zeros((tile_rows, lead, tiles * LANES), jnp.float32)

    received = {NORTH: got_n, SOUTH: got_s, EAST: got_e, WEST: got_w}
    for place, way in enumerate((NE, NW, SE, SW)):
        received[way] = got_corner.at[place]
    for way in range(8):

        @pl.when(jnp.logical_not(exists(way)))
        def _(way=way):
            received[way][...] = jnp.zeros(received[way].shape, jnp.float32)

    def planes_at(ref, t, group, r):
        at = group * SUB if isinstance(group, int) else pl.multiple_of(group * SUB, SUB)
        return ref[r, pl.ds(at, SUB), t * LANES : (t + 1) * LANES]

    def both_edges(first, last, spot_):
        return pltpu.roll(jnp.where(lane < PACK, first, last), PAIR * spot_ + PACK, 1)

    def gather_rows(source, group, at):
        for i in range(ITERS):
            for t in range(tiles):
                place = pl.ds(at + i * wide + t * SUB, SUB)
                rows_n[place, :] = planes_at(source, t, group, i)
                rows_s[place, :] = planes_at(source, t, group, tile_rows - ITERS + i)

    def put_columns(pieces, group, at):
        for n, source in enumerate(pieces):
            for third in range(thirds):
                value = jnp.zeros((SUB, LANES), jnp.float32)
                for spot_ in range(SLOTS):
                    r = third * SLOTS + spot_
                    moved = both_edges(
                        planes_at(source, 0, group, r),
                        planes_at(source, tiles - 1, group, r),
                        spot_,
                    )
                    value = jnp.where(block == spot_, moved, value)
                slab[pl.ds(at + (2 * third + n) * SUB, SUB), :] = value

    def fill_tables():
        def ramp(position, count, low_zone, high_zone):
            shape = position.shape
            scale_low = jnp.full(shape, (low_zone + 1).astype(jnp.float32))
            scale_high = jnp.full(shape, (high_zone + 1).astype(jnp.float32))
            lower = jnp.maximum(low_zone - position, 0).astype(jnp.float32) / scale_low
            upper = jnp.maximum(high_zone - (count - 1 - position), 0).astype(jnp.float32) / scale_high
            return jnp.maximum(lower, upper)

        row_index = row * tile_rows + lax.broadcasted_iota(jnp.int32, (tile_rows, LANES), 0)
        ramps[...] = ramp(row_index, tile_rows * nrow, zone_ref[0], zone_ref[1])
        tile_index = lax.broadcasted_iota(jnp.int32, (wide, LANES), 0) // SUB
        weight_cols = ramp(
            (col * tiles + tile_index) * LANES + lane_wide,
            tiles * LANES * ncol,
            zone_ref[2],
            zone_ref[3],
        )

        def weights(r, _):
            across = jnp.broadcast_to(ramps[pl.ds(r, 1), :], (wide, LANES))
            relaxation = jnp.maximum(across, weight_cols)
            at = pl.multiple_of(r * wide, SUB)
            keep[pl.ds(at, wide), :] = 1.0 - relaxation
            weigh[pl.ds(at, wide), :] = (1.0 - relaxation) / 9.0 + relaxation
            return 0

        lax.fori_loop(0, tile_rows, weights, 0, unroll=4)

        fine = lax.broadcasted_iota(jnp.int32, (tiles * LANES, LANES), 0)
        name = lax.broadcasted_iota(jnp.int32, (tiles * LANES, LANES), 1)
        pick[...] = (fine // 3 == name).astype(jnp.float32).astype(jnp.bfloat16)

        dests = [dest_ref[g] for g in range(coarse_rows)]
        from_lane = lax.broadcasted_iota(jnp.int32, (SUB, coarse_rows * SUB), 1)
        spot = jnp.zeros((SUB, coarse_rows * SUB), jnp.int32)
        for g in range(coarse_rows):
            rank = jnp.int32(0)
            for before in range(g):
                rank = rank + jnp.where(dests[before] == dests[g], 1, 0)
            spot = jnp.where(from_lane // SUB == g, dests[g] * CAP + rank, spot)
            tags[g * SUB : (g + 1) * SUB, :] = jnp.full(
                (SUB, LANES), (slot_ref[g] + 1).astype(jnp.float32)
            )
        same = from_lane % SUB == lax.broadcasted_iota(jnp.int32, (SUB, coarse_rows * SUB), 0)
        spot = jnp.where(same, spot, -1)
        for k in range(0, ncol * CAP, 2):
            pair = jnp.concatenate(
                [(spot == k).astype(jnp.float32), (spot == k + 1).astype(jnp.float32)], 0
            )
            route[k * SUB : (k + 2) * SUB, :] = pair.astype(jnp.bfloat16)

    sources = {NORTH: rows_n, SOUTH: rows_s}

    def remote(way, group, arriving=False, coefs=False):
        sent = OPPOSITE[way] if arriving else way
        back = OPPOSITE[sent]
        whole = per if sent < 2 else strip
        if sent >= 4:
            third = 0 if sent in (NE, NW) else thirds - 1
            count = 2 * SUB
            part = 0 if coefs else group + 1
            source = slab.at[pl.ds(aligned(part * strip + third * count), count), :]
            target = received[back].at[pl.ds(aligned(part * count), count), :]
        else:
            if isinstance(group, int) and group == 0:
                place = pl.ds(0, 2 * whole)
            else:
                place = pl.ds(aligned((group + 1) * whole), whole)
            source = sources.get(sent, slab).at[place, :]
            target = received[back].at[place, :]
        return pltpu.make_async_remote_copy(
            src_ref=source,
            dst_ref=target,
            send_sem=send_sem.at[sent],
            recv_sem=recv_sem.at[group * 8 + back],
            device_id=device(way),
            device_id_type=MESH,
        )

    def each(way, group, arriving=False):
        copies = [remote(way, group, arriving)]
        if way >= 4 and isinstance(group, int) and group == 0:
            copies.append(remote(way, group, arriving, True))
        return copies

    def greet():
        greeted = jnp.int32(ncol - 1)
        for way in GREETED:
            greeted = greeted + exists(way).astype(jnp.int32)
        pl.semaphore_wait(barrier, greeted)

    def send_halo(group):
        put_columns((field, spread), group, aligned((group + 1) * strip))
        if isinstance(group, int) and group == 0:
            greet()
        for way in (EAST, WEST, NE, NW, SE, SW):

            @pl.when(exists(way))
            def _(way=way):
                for copy in each(way, group):
                    copy.start()

        if isinstance(group, int) and group == 0:
            gather_rows(along_x, 0, 0)
            gather_rows(along_y, 0, ITERS * wide)
        at = aligned((group + 1) * per)
        gather_rows(field, group, at)
        gather_rows(spread, group, at + ITERS * wide)
        for way in (NORTH, SOUTH):

            @pl.when(exists(way))
            def _(way=way):
                for copy in each(way, group):
                    copy.start()

    def prepare(group):
        for n in range(2):
            wait_load(group, n)
        if isinstance(group, int):
            if group < orders:
                for n in range(2, len(arrays)):
                    wait_load(group, n)
        else:

            @pl.when(group < orders)
            def _():
                for n in range(2, len(arrays)):
                    wait_load(group, n)

        send_halo(group)

    for n in range(len(arrays)):
        wait_load(0, n)
    put_columns((along_x, along_y), 0, 0)
    send_halo(0)
    for later in range(1, groups):
        load_group(later)
    fill_tables()
    for later in range(1, min(AHEAD, groups)):
        prepare(later)

    def strip_of(array, base, corner_base, group_base):
        halo = jnp.zeros((SUB, LANES), jnp.float32)
        for got, first_slot in ((got_n, SLOTS - ITERS), (got_s, 0)):
            for i in range(ITERS):
                at = group_base + (array * ITERS + i) * wide
                moved = both_edges(
                    got[pl.ds(at, SUB), :],
                    got[pl.ds(at + (tiles - 1) * SUB, SUB), :],
                    first_slot + i,
                )
                halo = jnp.where(block == first_slot + i, moved, halo)

        def whole(ref, last):
            parts = [
                ref[pl.ds(base + (2 * third + array) * SUB, SUB), :] for third in range(thirds)
            ]
            return jnp.concatenate(parts + [last], 0)

        own = whole(slab, halo)
        out = []
        for side, got in enumerate((got_e, got_w)):
            corner = pl.ds(corner_base + array * SUB, SUB)
            last = jnp.where(
                block >= SLOTS - ITERS, got_corner[side, corner, :], got_corner[2 + side, corner, :]
            )
            last = jnp.where(
                jnp.logical_or(block >= SLOTS - ITERS, block < ITERS), last, jnp.zeros_like(last)
            )
            other = whole(got, last)
            west, east = (own, other) if side == 0 else (other, own)
            out.append(jnp.where(inner < PACK, west, east))
        return out

    def variants(value):
        sub = lax.broadcasted_iota(jnp.int32, (SUB, LANES), 0)
        out = []
        for group in range(groups):
            shift = (group * SUB) % levels
            if shift == 0:
                out.append(value)
            else:
                out.append(
                    jnp.where(
                        sub + shift < SUB,
                        pltpu.roll(value, SUB - shift, 0),
                        pltpu.roll(value, levels - shift, 0),
                    )
                )
        return out

    def wait_halo(group):
        for way in range(8):

            @pl.when(exists(way))
            def _(way=way):
                if way >= 4 and isinstance(group, int) and group == 0:
                    region = received[way].at[0 : 4 * SUB, :]
                    pltpu.make_async_copy(region, region, recv_sem.at[way]).wait()
                else:
                    remote(way, group, True).wait_recv()

    def share_coefs():
        for which, got in enumerate((got_n, got_s)):

            def one(n, _, got=got, which=which):
                at = pl.multiple_of(n * SUB, SUB)
                for group, value in enumerate(variants(got[pl.ds(at, SUB), :])):
                    halo_coef[group, which, pl.ds(at, SUB), :] = value
                return 0

            lax.fori_loop(0, per // SUB, one, 0, unroll=6)
        for array in range(2):
            for side, value in enumerate(strip_of(array, 0, 0, 0)):
                for third in range(thirds + 1):
                    at = (array * (thirds + 1) + third) * SUB
                    part = value[third * SUB : (third + 1) * SUB]
                    for group, moved in enumerate(variants(part)):
                        edge_coef[group, side, at : at + SUB, :] = moved

    def products(v, d, along, across):
        w = 0.5 * v
        p, x, y = d * v, along * w, across * w
        return v - 4.0 * p, p + x, p - x, p + y, p - y

    def next_rows(value):
        moved = pltpu.roll(value, PAIR, 1)
        carried = jnp.concatenate([moved[thirds * SUB :], moved[: thirds * SUB]], 0)
        return jnp.where(lane_strip < PAIR, carried, moved)

    def previous_rows(value):
        moved = pltpu.roll(value, LANES - PAIR, 1)
        carried = jnp.concatenate([moved[SUB:], moved[:SUB]], 0)
        return jnp.where(lane_strip >= LANES - PAIR, carried, moved)

    def strips(group):
        base = pl.multiple_of((group + 1) * strip, SUB)
        corner_base = pl.multiple_of((group + 1) * 2 * SUB, SUB)
        group_base = pl.multiple_of((group + 1) * per, SUB)
        fields_now = strip_of(0, base, corner_base, group_base)
        spreads = strip_of(1, base, corner_base, group_base)
        count = (thirds + 1) * SUB
        flux = []
        for side in range(2):
            now, d = fields_now[side], spreads[side]
            hx = edge_coef[group, side, 0:count, :]
            hy = edge_coef[group, side, count : 2 * count, :]
            flux.append([])
            for sweep in range(ITERS):
                center, up, down, right, left = products(now, d, hx, hy)
                flux[side].append(right if side == 0 else left)
                if sweep < ITERS - 1:
                    now = (
                        center
                        + previous_rows(up)
                        + next_rows(down)
                        + (pltpu.roll(right, LANES - 1, 1) + pltpu.roll(left, 1, 1))
                    )
        for sweep in range(ITERS):
            edges[sweep] = jnp.where(
                inner == PACK, flux[0][sweep], pltpu.roll(flux[1][sweep], 2, 1)
            )

    def march(group):
        order = lax.rem(group, orders)
        at_last, at_first = lane_wide == LANES - 1, lane_wide == 0

        def row_of(ref, r, which):
            return jnp.concatenate([planes_at(ref, t, which, r) for t in range(tiles)], 0)

        def coefs(r):
            if 0 <= r < tile_rows:
                return (
                    row_of(spread, r, group),
                    row_of(along_x, r, order),
                    row_of(along_y, r, order),
                )
            which, i = (0, r + ITERS) if r < 0 else (1, r - tile_rows)
            base = pl.multiple_of((group + 1) * per, SUB)
            d = (got_n, got_s)[which][pl.ds(base + (ITERS + i) * wide, wide), :]
            along = halo_coef[group, which, i * wide : (i + 1) * wide, :]
            across = halo_coef[group, which, (ITERS + i) * wide : (ITERS + i + 1) * wide, :]
            return d, along, across

        def value(sweep, r):
            if sweep > 0:
                return between[sweep - 1, (r + ITERS) * wide : (r + ITERS + 1) * wide, :]
            if 0 <= r < tile_rows:
                return row_of(field, r, group)
            which, i = (0, r + ITERS) if r < 0 else (1, r - tile_rows)
            base = pl.multiple_of((group + 1) * per, SUB)
            return (got_n, got_s)[which][pl.ds(base + i * wide, wide), :]

        def lateral(right, left, sweep, r):
            part, spot_ = divmod(r % ((thirds + 1) * SLOTS), SLOTS)
            beyond = pltpu.roll(
                edges[sweep, part * SUB : (part + 1) * SUB, :],
                LANES - 1 - PACK - PAIR * spot_,
                1,
            )
            right, left = pltpu.roll(right, LANES - 1, 1), pltpu.roll(left, 1, 1)
            from_right = jnp.concatenate([right[SUB:], beyond], 0)
            from_left = jnp.concatenate([beyond, left[: wide - SUB]], 0)
            return jnp.where(at_last, from_right, right) + jnp.where(at_first, from_left, left)

        def finish_row(r, v):
            at = r * wide if isinstance(r, int) else pl.multiple_of(r * wide, SUB)
            out = keep[pl.ds(at, wide), :] * v
            for t in range(tiles):
                place = pl.ds(pl.multiple_of(group * SUB, SUB), SUB)
                nest[r, place, t * LANES : (t + 1) * LANES] = out[t * SUB : (t + 1) * SUB]
            return weigh[pl.ds(at, wide), :] * v

        def put_sum(g, value):
            at = g * SUB if isinstance(g, int) else pl.multiple_of(g * SUB, SUB)
            for t in range(tiles):
                sums[pl.ds(at, SUB), t * LANES : (t + 1) * LANES] = value[t * SUB : (t + 1) * SUB]

        total = None
        for sweep in range(ITERS):
            reach = ITERS - 1 - sweep
            base, sideways, down = None, None, None
            for r in range(-reach - 1, tile_rows + reach + 1):
                v = value(sweep, r)
                d, along, across = coefs(r)
                if r == -reach - 1:
                    down = d * v - along * (0.5 * v)
                    continue
                if r == tile_rows + reach:
                    up = d * v + along * (0.5 * v)
                else:
                    center, up, below, right, left = products(v, d, along, across)
                done = r - 1
                if done >= -reach:
                    result = (base + up) + sideways
                    if sweep < ITERS - 1:
                        between[sweep, (done + ITERS) * wide : (done + ITERS + 1) * wide, :] = result
                    else:
                        term = finish_row(done, result)
                        total = term if done % 3 == 0 else total + term
                        if done % 3 == 2:
                            put_sum(done // 3, total)
                if r < tile_rows + reach:
                    base = center + down
                    sideways = lateral(right, left, sweep, r)
                    down = below

    def to_owner(group, step):
        owner = lax.rem(col + step, ncol)
        rows = CAP * SUB
        return pltpu.make_async_remote_copy(
            src_ref=outbound.at[group, owner],
            dst_ref=arrived.at[group, pl.ds(step * rows, rows), :],
            send_sem=out_sem.at[0],
            recv_sem=in_sem.at[group],
            device_id=(row, owner),
            device_id_type=MESH,
        )

    tag_row = lax.broadcasted_iota(jnp.int32, (coarse_rows * SUB, LANES), 0) % SUB == 0

    def one_group(group, _):
        @pl.when(group + AHEAD < groups)
        def _():
            prepare(group + AHEAD)

        @pl.when(group > 0)
        def _():
            wait_halo(group)

        @pl.when(group == 0)
        def _():
            wait_halo(0)
            share_coefs()

        strips(group)
        march(group)
        high, low = split(sums[...])
        coarse = dot(high, pick[...]) + dot(low, pick[...])
        coarse = jnp.where(jnp.logical_and(tag_row, group == 0), tags[...], coarse)
        high, low = split(coarse)
        routed = dot(route[...], high) + dot(route[...], low)
        for k in range(ncol):
            outbound[group, k] = routed[k * CAP * SUB : (k + 1) * CAP * SUB]
        for step in range(1, ncol):
            to_owner(group, step).start()
        arrived[group, 0 : CAP * SUB, :] = outbound[group, col]
        return 0

    lax.fori_loop(0, groups, one_group, 0)

    for way in range(8):

        @pl.when(exists(way))
        def _(way=way):
            pltpu.make_async_copy(received[way], received[way], send_sem.at[way]).wait()

    sent_away = outbound.at[:, 1:ncol]
    pltpu.make_async_copy(sent_away, sent_away, out_sem.at[0]).wait()

    count = ncol * CAP
    filler = jnp.zeros((LANES - 2 * count, LANES), jnp.bfloat16)
    for group in range(groups):
        region = arrived.at[group, CAP * SUB : ncol * CAP * SUB, :]
        pltpu.make_async_copy(region, region, in_sem.at[group]).wait()
        if group == 0:
            named = arrived[0, pl.ds(0, count, stride=SUB), :]
            lines = lax.broadcasted_iota(jnp.int32, (count, LANES), 1).astype(jnp.float32) + 1.0
            picked = (named == lines).astype(jnp.float32)
            stack = jnp.concatenate(
                [picked, picked, jnp.zeros((LANES - 2 * count, LANES), jnp.float32)], 0
            )
            picker = stack.T[:PROWS].astype(jnp.bfloat16)
        for place in range(group * SUB, (group + 1) * SUB):
            if place >= lead:
                high, low = split(arrived[group, pl.ds(place % SUB, count, stride=SUB), :])
                parent[place - lead] = dot(picker, jnp.concatenate([high, low, filler], 0))


def finish(dims, nest, parent, nest_hbm, parent_hbm, store_sem):
    fields, levels, tile_rows = dims
    planes = fields * levels
    lead = round_up(planes + 1, SUB) - planes
    whole = pltpu.make_async_copy(parent, parent_hbm, store_sem.at[1])
    whole.start()
    for p in range(planes):
        pltpu.make_async_copy(
            nest.at[:, lead + p, :],
            nest_hbm.at[p * tile_rows : (p + 1) * tile_rows, :],
            store_sem.at[0],
        ).start()
    pltpu.make_async_copy(nest_hbm, nest_hbm, store_sem.at[0]).wait()
    whole.wait()


def shards(adjoint_field, advect_x, advect_y, diffusion, zone_cells, feedback_dest, feedback_slot):
    fields, levels, tile_rows, tile_cols = adjoint_field.shape
    planes = fields * levels
    tiles = tile_cols // LANES
    ncol = lax.axis_size("col")
    padded = round_up(planes + 1, SUB)
    groups = padded // SUB
    orders = variants_of(groups, levels)
    thirds = tile_rows * PAIR // LANES
    coarse_rows = tile_rows // 3
    wide = tiles * SUB
    f32 = jnp.float32
    vmem = pltpu.VMEM
    dma = pltpu.SemaphoreType.DMA
    smem_spec = pl.BlockSpec(memory_space=pltpu.SMEM)
    any_spec = pl.BlockSpec(memory_space=pl.ANY)
    vmem_spec = pl.BlockSpec(memory_space=pltpu.VMEM)
    own = (tile_rows, padded, tile_cols)
    level_own = (tile_rows, orders * SUB, tile_cols)
    halo_rows = ((groups + 1) * 2 * ITERS * wide, LANES)
    halo_cols = ((groups + 1) * thirds * 2 * SUB, LANES)
    halo_corner = (groups + 1) * 2 * SUB
    nest, parent = pl.pallas_call(
        functools.partial(kernel, (fields, levels, tile_rows, tiles)),
        out_shape=[
            pltpu.VMEM(own, f32),
            pltpu.VMEM((planes, PROWS, LANES), f32),
        ],
        in_specs=[smem_spec] * 3 + [any_spec] * 4,
        out_specs=[vmem_spec] * 2,
        scratch_shapes=[
            vmem((groups, ncol * CAP * SUB, LANES), f32),
            vmem(own, f32),
            vmem(own, f32),
            vmem(level_own, f32),
            vmem(level_own, f32),
            vmem((tile_rows, LANES), f32),
            vmem((tile_rows * wide, LANES), f32),
            vmem((tile_rows * wide, LANES), f32),
            vmem((coarse_rows * SUB, tiles * LANES), f32),
            vmem((tiles * LANES, LANES), jnp.bfloat16),
            vmem((ncol * CAP * SUB, coarse_rows * SUB), jnp.bfloat16),
            vmem((coarse_rows * SUB, LANES), f32),
            vmem((groups, ncol, CAP * SUB, LANES), f32),
        ]
        + [vmem(halo_rows, f32)] * 4
        + [vmem(halo_cols, f32)] * 3
        + [
            vmem((4, halo_corner, LANES), f32),
            vmem((groups, 2, 2 * ITERS * wide, LANES), f32),
            vmem((groups, 2, 2 * (thirds + 1) * SUB, LANES), f32),
            vmem((ITERS, (thirds + 1) * SUB, LANES), f32),
            vmem((ITERS - 1, (tile_rows + 2 * ITERS) * wide, LANES), f32),
            dma((4 * groups,)),
            dma((8,)),
            dma((8 * groups,)),
            dma((1,)),
            dma((groups,)),
        ],
        compiler_params=pltpu.CompilerParams(
            collective_id=0, has_side_effects=True, vmem_limit_bytes=60 * 1024 * 1024
        ),
    )(
        zone_cells,
        feedback_dest.reshape(-1),
        feedback_slot.reshape(-1),
        adjoint_field.reshape(planes * tile_rows, tile_cols),
        diffusion.reshape(planes * tile_rows, tile_cols),
        advect_x.reshape(levels * tile_rows, tile_cols),
        advect_y.reshape(levels * tile_rows, tile_cols),
    )
    nest, parent = pl.pallas_call(
        functools.partial(finish, (fields, levels, tile_rows)),
        out_shape=(
            jax.ShapeDtypeStruct((planes * tile_rows, tile_cols), f32),
            jax.ShapeDtypeStruct((planes, PROWS, LANES), f32),
        ),
        in_specs=[vmem_spec] * 2,
        out_specs=(any_spec, any_spec),
        scratch_shapes=[dma((2,))],
        compiler_params=pltpu.CompilerParams(vmem_limit_bytes=16 * 1024 * 1024),
    )(nest, parent)
    return (
        nest.reshape(adjoint_field.shape),
        parent.reshape(fields, levels, PROWS, LANES),
    )


def solution(mesh):
    placed = (
        P(None, None, "row", "col"),
        P(None, "row", "col"),
        P(None, "row", "col"),
        P(None, None, "row", "col"),
        P(),
        P("col", "row", None),
        P("col", "row", None),
    )
    return jax.shard_map(
        shards,
        mesh=mesh,
        in_specs=placed,
        out_specs=(P(None, None, "row", "col"), P(None, None, "row", "col")),
        check_vma=False,
    )
```

```python
import functools
import math

import jax
import jax.numpy as jnp
from jax import lax
from jax.experimental import pallas as pl
from jax.experimental.pallas import tpu as pltpu
from jax.sharding import PartitionSpec as P

ITERS = 3
PROWS = 80
CAP = 2
LANES = 128
SUB = 8
PACK = 4
PAIR = 2 * PACK
AHEAD = 2
SLOTS = LANES // PAIR
MESH = pl.DeviceIdType.MESH
DIRS = ((-1, 0), (1, 0), (0, 1), (0, -1), (-1, 1), (-1, -1), (1, 1), (1, -1))
NORTH, SOUTH, EAST, WEST, NE, NW, SE, SW = range(8)
OPPOSITE = (SOUTH, NORTH, WEST, EAST, SW, SE, NW, NE)
GREETED = (NORTH, SOUTH, NE, NW, SE, SW)


def round_up(value, step):
    return -(-value // step) * step


def split(values):
    high = values.astype(jnp.bfloat16)
    return high, (values - high.astype(jnp.float32)).astype(jnp.bfloat16)


def dot(left, right):
    return jnp.dot(left, right, preferred_element_type=jnp.float32)


def variants_of(groups, levels):
    return min(groups, levels // math.gcd(levels, SUB))


def kernel(
    dims,
    zone_ref,
    dest_ref,
    slot_ref,
    field_hbm,
    spread_hbm,
    along_x_hbm,
    along_y_hbm,
    nest,
    parent,
    arrived,
    field,
    spread,
    along_x,
    along_y,
    ramps,
    keep,
    weigh,
    sums,
    pick,
    route,
    tags,
    outbound,
    rows_n,
    rows_s,
    got_n,
    got_s,
    slab,
    msg_e,
    msg_w,
    got_e,
    got_w,
    got_corner,
    halo_coef,
    edge_coef,
    edges,
    between,
    load_sem,
    send_sem,
    recv_sem,
    out_sem,
    in_sem,
):
    fields, levels, tile_rows, tiles = dims
    planes = fields * levels
    padded = round_up(planes + 1, SUB)
    groups, lead = padded // SUB, padded - planes
    wide = tiles * SUB
    per = 2 * ITERS * wide
    row, col = lax.axis_index("row"), lax.axis_index("col")
    nrow, ncol = lax.axis_size("row"), lax.axis_size("col")
    coarse_rows = tile_rows // 3

    def exists(way):
        down, over = DIRS[way]
        conditions = []
        if down < 0:
            conditions.append(row > 0)
        if down > 0:
            conditions.append(row < nrow - 1)
        if over < 0:
            conditions.append(col > 0)
        if over > 0:
            conditions.append(col < ncol - 1)
        return functools.reduce(jnp.logical_and, conditions)

    def device(way):
        return (row + DIRS[way][0], col + DIRS[way][1])

    def aligned(value):
        return value if isinstance(value, int) else pl.multiple_of(value, SUB)

    orders = variants_of(groups, levels)
    thirds = tile_rows // SLOTS
    strip = thirds * 2 * SUB
    arrays = ((field_hbm, field), (spread_hbm, spread), (along_x_hbm, along_x), (along_y_hbm, along_y))

    def load_group(group):
        for place in range(group * SUB, (group + 1) * SUB):
            for n, (source, target) in enumerate(arrays):
                if n < 2 and place < lead or n >= 2 and group >= orders:
                    continue
                number = place - lead if n < 2 else (place - lead) % levels
                pltpu.make_async_copy(
                    source.at[number * tile_rows : (number + 1) * tile_rows, :],
                    target.at[:, place, :],
                    load_sem.at[group * len(arrays) + n],
                ).start()

    def wait_load(group, n):
        target = arrays[n][1]
        if isinstance(group, int):
            first = max(group * SUB, lead) if n < 2 else group * SUB
            region = target.at[:, first : (group + 1) * SUB, :]
        else:
            region = target.at[:, pl.ds(aligned(group * SUB), SUB), :]
        pltpu.make_async_copy(region, region, load_sem.at[group * len(arrays) + n]).wait()

    load_group(0)

    barrier = pltpu.get_barrier_semaphore()
    for way in GREETED:

        @pl.when(exists(way))
        def _(way=way):
            pl.semaphore_signal(barrier, inc=1, device_id=device(way), device_id_type=MESH)

    for step in range(1, ncol):
        pl.semaphore_signal(
            barrier, inc=1, device_id=(row, lax.rem(col + step, ncol)), device_id_type=MESH
        )

    lane = lax.broadcasted_iota(jnp.int32, (SUB, LANES), 1)
    block = lane // PAIR
    lane_wide = lax.broadcasted_iota(jnp.int32, (wide, LANES), 1)
    lane_strip = lax.broadcasted_iota(jnp.int32, ((thirds + 1) * SUB, LANES), 1)
    inner = lane_strip % PAIR

    for ref in (field, spread):
        ref[:, 0:lead, :] = jnp.zeros((tile_rows, lead, tiles * LANES), jnp.float32)

    received = {NORTH: got_n, SOUTH: got_s, EAST: got_e, WEST: got_w}
    for place, way in enumerate((NE, NW, SE, SW)):
        received[way] = got_corner.at[place]
    for way in range(8):

        @pl.when(jnp.logical_not(exists(way)))
        def _(way=way):
            received[way][...] = jnp.zeros(received[way].shape, jnp.float32)

    def planes_at(ref, t, group, r):
        at = group * SUB if isinstance(group, int) else pl.multiple_of(group * SUB, SUB)
        return ref[r, pl.ds(at, SUB), t * LANES : (t + 1) * LANES]

    def both_edges(first, last, spot_):
        return pltpu.roll(jnp.where(lane < PACK, first, last), PAIR * spot_ + PACK, 1)

    def gather_rows(source, group, at):
        for i in range(ITERS):
            for t in range(tiles):
                place = pl.ds(at + i * wide + t * SUB, SUB)
                rows_n[place, :] = planes_at(source, t, group, i)
                rows_s[place, :] = planes_at(source, t, group, tile_rows - ITERS + i)

    def put_columns(pieces, group, at):
        for n, source in enumerate(pieces):
            for third in range(thirds):
                value = jnp.zeros((SUB, LANES), jnp.float32)
                for spot_ in range(SLOTS):
                    r = third * SLOTS + spot_
                    moved = both_edges(
                        planes_at(source, 0, group, r),
                        planes_at(source, tiles - 1, group, r),
                        spot_,
                    )
                    value = jnp.where(block == spot_, moved, value)
                slab[pl.ds(at + (2 * third + n) * SUB, SUB), :] = value

    def fill_tables():
        def ramp(position, count, low_zone, high_zone):
            shape = position.shape
            scale_low = jnp.full(shape, (low_zone + 1).astype(jnp.float32))
            scale_high = jnp.full(shape, (high_zone + 1).astype(jnp.float32))
            lower = jnp.maximum(low_zone - position, 0).astype(jnp.float32) / scale_low
            upper = jnp.maximum(high_zone - (count - 1 - position), 0).astype(jnp.float32) / scale_high
            return jnp.maximum(lower, upper)

        row_index = row * tile_rows + lax.broadcasted_iota(jnp.int32, (tile_rows, LANES), 0)
        ramps[...] = ramp(row_index, tile_rows * nrow, zone_ref[0], zone_ref[1])
        tile_index = lax.broadcasted_iota(jnp.int32, (wide, LANES), 0) // SUB
        weight_cols = ramp(
            (col * tiles + tile_index) * LANES + lane_wide,
            tiles * LANES * ncol,
            zone_ref[2],
            zone_ref[3],
        )

        def weights(r, _):
            across = jnp.broadcast_to(ramps[pl.ds(r, 1), :], (wide, LANES))
            relaxation = jnp.maximum(across, weight_cols)
            at = pl.multiple_of(r * wide, SUB)
            keep[pl.ds(at, wide), :] = 1.0 - relaxation
            weigh[pl.ds(at, wide), :] = (1.0 - relaxation) / 9.0 + relaxation
            return 0

        lax.fori_loop(0, tile_rows, weights, 0, unroll=4)

        fine = lax.broadcasted_iota(jnp.int32, (tiles * LANES, LANES), 0)
        name = lax.broadcasted_iota(jnp.int32, (tiles * LANES, LANES), 1)
        pick[...] = (fine // 3 == name).astype(jnp.float32).astype(jnp.bfloat16)

        dests = [dest_ref[g] for g in range(coarse_rows)]
        from_lane = lax.broadcasted_iota(jnp.int32, (SUB, coarse_rows * SUB), 1)
        spot = jnp.zeros((SUB, coarse_rows * SUB), jnp.int32)
        for g in range(coarse_rows):
            rank = jnp.int32(0)
            for before in range(g):
                rank = rank + jnp.where(dests[before] == dests[g], 1, 0)
            spot = jnp.where(from_lane // SUB == g, dests[g] * CAP + rank, spot)
            tags[g * SUB : (g + 1) * SUB, :] = jnp.full(
                (SUB, LANES), (slot_ref[g] + 1).astype(jnp.float32)
            )
        same = from_lane % SUB == lax.broadcasted_iota(jnp.int32, (SUB, coarse_rows * SUB), 0)
        spot = jnp.where(same, spot, -1)
        for k in range(0, ncol * CAP, 2):
            pair = jnp.concatenate(
                [(spot == k).astype(jnp.float32), (spot == k + 1).astype(jnp.float32)], 0
            )
            route[k * SUB : (k + 2) * SUB, :] = pair.astype(jnp.bfloat16)

    first_half = lane % PAIR < PACK

    def put_messages(part):
        base, to = aligned(part * strip), aligned(part * thirds * SUB)
        units = [
            slab[pl.ds(base + (2 * third + n) * SUB, SUB), :]
            for n in range(2)
            for third in range(thirds)
        ]
        for i in range(thirds):
            one, two = units[2 * i], units[2 * i + 1]
            place = pl.ds(to + i * SUB, SUB)
            msg_e[place, :] = jnp.where(first_half, one, pltpu.roll(two, PACK, 1))
            msg_w[place, :] = jnp.where(first_half, pltpu.roll(one, LANES - PACK, 1), two)

    sources = {NORTH: rows_n, SOUTH: rows_s, EAST: msg_e, WEST: msg_w}

    def remote(way, group, arriving=False, coefs=False):
        sent = OPPOSITE[way] if arriving else way
        back = OPPOSITE[sent]
        whole = per if sent < 2 else thirds * SUB
        if sent >= 4:
            third = 0 if sent in (NE, NW) else thirds - 1
            count = 2 * SUB
            part = 0 if coefs else group + 1
            source = slab.at[pl.ds(aligned(part * strip + third * count), count), :]
            target = received[back].at[pl.ds(aligned(part * count), count), :]
        else:
            if isinstance(group, int) and group == 0:
                place = pl.ds(0, 2 * whole)
            else:
                place = pl.ds(aligned((group + 1) * whole), whole)
            source = sources[sent].at[place, :]
            target = received[back].at[place, :]
        return pltpu.make_async_remote_copy(
            src_ref=source,
            dst_ref=target,
            send_sem=send_sem.at[sent],
            recv_sem=recv_sem.at[group * 8 + back],
            device_id=device(way),
            device_id_type=MESH,
        )

    def each(way, group, arriving=False):
        copies = [remote(way, group, arriving)]
        if way >= 4 and isinstance(group, int) and group == 0:
            copies.append(remote(way, group, arriving, True))
        return copies

    def greet():
        greeted = jnp.int32(ncol - 1)
        for way in GREETED:
            greeted = greeted + exists(way).astype(jnp.int32)
        pl.semaphore_wait(barrier, greeted)

    def send_halo(group):
        put_columns((field, spread), group, aligned((group + 1) * strip))
        put_messages(group + 1)
        if isinstance(group, int) and group == 0:
            greet()
        for way in (EAST, WEST, NE, NW, SE, SW):

            @pl.when(exists(way))
            def _(way=way):
                for copy in each(way, group):
                    copy.start()

        if isinstance(group, int) and group == 0:
            gather_rows(along_x, 0, 0)
            gather_rows(along_y, 0, ITERS * wide)
        at = aligned((group + 1) * per)
        gather_rows(field, group, at)
        gather_rows(spread, group, at + ITERS * wide)
        for way in (NORTH, SOUTH):

            @pl.when(exists(way))
            def _(way=way):
                for copy in each(way, group):
                    copy.start()

    def prepare(group):
        for n in range(2):
            wait_load(group, n)
        if isinstance(group, int):
            if group < orders:
                for n in range(2, len(arrays)):
                    wait_load(group, n)
        else:

            @pl.when(group < orders)
            def _():
                for n in range(2, len(arrays)):
                    wait_load(group, n)

        send_halo(group)

    for n in range(len(arrays)):
        wait_load(0, n)
    put_columns((along_x, along_y), 0, 0)
    put_messages(0)
    send_halo(0)
    for later in range(1, groups):
        load_group(later)
    fill_tables()
    for later in range(1, min(AHEAD, groups)):
        prepare(later)

    def strip_of(array, base, message_base, corner_base, group_base):
        halo = jnp.zeros((SUB, LANES), jnp.float32)
        for got, first_slot in ((got_n, SLOTS - ITERS), (got_s, 0)):
            for i in range(ITERS):
                at = group_base + (array * ITERS + i) * wide
                moved = both_edges(
                    got[pl.ds(at, SUB), :],
                    got[pl.ds(at + (tiles - 1) * SUB, SUB), :],
                    first_slot + i,
                )
                halo = jnp.where(block == first_slot + i, moved, halo)

        def unpacked(got, side, third):
            pair, second = divmod(array * thirds + third, 2)
            value = got[pl.ds(message_base + pair * SUB, SUB), :]
            if side == 0:
                return value if second else pltpu.roll(value, PACK, 1)
            return pltpu.roll(value, LANES - PACK, 1) if second else value

        parts = [slab[pl.ds(base + (2 * third + array) * SUB, SUB), :] for third in range(thirds)]
        own = jnp.concatenate(parts + [halo], 0)
        out = []
        for side, got in enumerate((got_e, got_w)):
            corner = pl.ds(corner_base + array * SUB, SUB)
            last = jnp.where(
                block >= SLOTS - ITERS, got_corner[side, corner, :], got_corner[2 + side, corner, :]
            )
            last = jnp.where(
                jnp.logical_or(block >= SLOTS - ITERS, block < ITERS), last, jnp.zeros_like(last)
            )
            parts = [unpacked(got, side, third) for third in range(thirds)]
            other = jnp.concatenate(parts + [last], 0)
            west, east = (own, other) if side == 0 else (other, own)
            out.append(jnp.where(inner < PACK, west, east))
        return out

    def variants(value):
        sub = lax.broadcasted_iota(jnp.int32, (SUB, LANES), 0)
        out = []
        for group in range(groups):
            shift = (group * SUB) % levels
            if shift == 0:
                out.append(value)
            else:
                out.append(
                    jnp.where(
                        sub + shift < SUB,
                        pltpu.roll(value, SUB - shift, 0),
                        pltpu.roll(value, levels - shift, 0),
                    )
                )
        return out

    def wait_halo(group):
        for way in range(8):

            @pl.when(exists(way))
            def _(way=way):
                if way >= 4 and isinstance(group, int) and group == 0:
                    region = received[way].at[0 : 4 * SUB, :]
                    pltpu.make_async_copy(region, region, recv_sem.at[way]).wait()
                else:
                    remote(way, group, True).wait_recv()

    def share_coefs():
        for which, got in enumerate((got_n, got_s)):

            def one(n, _, got=got, which=which):
                at = pl.multiple_of(n * SUB, SUB)
                for group, value in enumerate(variants(got[pl.ds(at, SUB), :])):
                    halo_coef[group, which, pl.ds(at, SUB), :] = value
                return 0

            lax.fori_loop(0, per // SUB, one, 0, unroll=6)
        for array in range(2):
            for side, value in enumerate(strip_of(array, 0, 0, 0, 0)):
                for third in range(thirds + 1):
                    at = (array * (thirds + 1) + third) * SUB
                    part = value[third * SUB : (third + 1) * SUB]
                    for group, moved in enumerate(variants(part)):
                        edge_coef[group, side, at : at + SUB, :] = moved

    def products(v, d, along, across):
        w = 0.5 * v
        p, x, y = d * v, along * w, across * w
        return v - 4.0 * p, p + x, p - x, p + y, p - y

    def next_rows(value):
        moved = pltpu.roll(value, PAIR, 1)
        carried = jnp.concatenate([moved[thirds * SUB :], moved[: thirds * SUB]], 0)
        return jnp.where(lane_strip < PAIR, carried, moved)

    def previous_rows(value):
        moved = pltpu.roll(value, LANES - PAIR, 1)
        carried = jnp.concatenate([moved[SUB:], moved[:SUB]], 0)
        return jnp.where(lane_strip >= LANES - PAIR, carried, moved)

    def strips(group):
        base = pl.multiple_of((group + 1) * strip, SUB)
        message_base = pl.multiple_of((group + 1) * thirds * SUB, SUB)
        corner_base = pl.multiple_of((group + 1) * 2 * SUB, SUB)
        group_base = pl.multiple_of((group + 1) * per, SUB)
        fields_now = strip_of(0, base, message_base, corner_base, group_base)
        spreads = strip_of(1, base, message_base, corner_base, group_base)
        count = (thirds + 1) * SUB
        flux = []
        for side in range(2):
            now, d = fields_now[side], spreads[side]
            hx = edge_coef[group, side, 0:count, :]
            hy = edge_coef[group, side, count : 2 * count, :]
            flux.append([])
            for sweep in range(ITERS):
                center, up, down, right, left = products(now, d, hx, hy)
                flux[side].append(right if side == 0 else left)
                if sweep < ITERS - 1:
                    now = (
                        center
                        + previous_rows(up)
                        + next_rows(down)
                        + (pltpu.roll(right, LANES - 1, 1) + pltpu.roll(left, 1, 1))
                    )
        for sweep in range(ITERS):
            edges[sweep] = jnp.where(
                inner == PACK, flux[0][sweep], pltpu.roll(flux[1][sweep], 2, 1)
            )

    def march(group):
        order = lax.rem(group, orders)
        at_last, at_first = lane_wide == LANES - 1, lane_wide == 0

        def row_of(ref, r, which):
            return jnp.concatenate([planes_at(ref, t, which, r) for t in range(tiles)], 0)

        def coefs(r):
            if 0 <= r < tile_rows:
                return (
                    row_of(spread, r, group),
                    row_of(along_x, r, order),
                    row_of(along_y, r, order),
                )
            which, i = (0, r + ITERS) if r < 0 else (1, r - tile_rows)
            base = pl.multiple_of((group + 1) * per, SUB)
            d = (got_n, got_s)[which][pl.ds(base + (ITERS + i) * wide, wide), :]
            along = halo_coef[group, which, i * wide : (i + 1) * wide, :]
            across = halo_coef[group, which, (ITERS + i) * wide : (ITERS + i + 1) * wide, :]
            return d, along, across

        def value(sweep, r):
            if sweep > 0:
                return between[sweep - 1, (r + ITERS) * wide : (r + ITERS + 1) * wide, :]
            if 0 <= r < tile_rows:
                return row_of(field, r, group)
            which, i = (0, r + ITERS) if r < 0 else (1, r - tile_rows)
            base = pl.multiple_of((group + 1) * per, SUB)
            return (got_n, got_s)[which][pl.ds(base + i * wide, wide), :]

        def lateral(right, left, sweep, r):
            part, spot_ = divmod(r % ((thirds + 1) * SLOTS), SLOTS)
            beyond = pltpu.roll(
                edges[sweep, part * SUB : (part + 1) * SUB, :],
                LANES - 1 - PACK - PAIR * spot_,
                1,
            )
            right, left = pltpu.roll(right, LANES - 1, 1), pltpu.roll(left, 1, 1)
            from_right = jnp.concatenate([right[SUB:], beyond], 0)
            from_left = jnp.concatenate([beyond, left[: wide - SUB]], 0)
            return jnp.where(at_last, from_right, right) + jnp.where(at_first, from_left, left)

        def finish_row(r, v):
            at = r * wide if isinstance(r, int) else pl.multiple_of(r * wide, SUB)
            out = keep[pl.ds(at, wide), :] * v
            for t in range(tiles):
                place = pl.ds(pl.multiple_of(group * SUB, SUB), SUB)
                nest[r, place, t * LANES : (t + 1) * LANES] = out[t * SUB : (t + 1) * SUB]
            return weigh[pl.ds(at, wide), :] * v

        def put_sum(g, value):
            at = g * SUB if isinstance(g, int) else pl.multiple_of(g * SUB, SUB)
            for t in range(tiles):
                sums[pl.ds(at, SUB), t * LANES : (t + 1) * LANES] = value[t * SUB : (t + 1) * SUB]

        total = None
        for sweep in range(ITERS):
            reach = ITERS - 1 - sweep
            base, sideways, down = None, None, None
            for r in range(-reach - 1, tile_rows + reach + 1):
                v = value(sweep, r)
                d, along, across = coefs(r)
                if r == -reach - 1:
                    down = d * v - along * (0.5 * v)
                    continue
                if r == tile_rows + reach:
                    up = d * v + along * (0.5 * v)
                else:
                    center, up, below, right, left = products(v, d, along, across)
                done = r - 1
                if done >= -reach:
                    result = (base + up) + sideways
                    if sweep < ITERS - 1:
                        between[sweep, (done + ITERS) * wide : (done + ITERS + 1) * wide, :] = result
                    else:
                        term = finish_row(done, result)
                        total = term if done % 3 == 0 else total + term
                        if done % 3 == 2:
                            put_sum(done // 3, total)
                if r < tile_rows + reach:
                    base = center + down
                    sideways = lateral(right, left, sweep, r)
                    down = below

    def to_owner(group, step):
        owner = lax.rem(col + step, ncol)
        rows = CAP * SUB
        return pltpu.make_async_remote_copy(
            src_ref=outbound.at[group, owner],
            dst_ref=arrived.at[group, pl.ds(step * rows, rows), :],
            send_sem=out_sem.at[0],
            recv_sem=in_sem.at[group],
            device_id=(row, owner),
            device_id_type=MESH,
        )

    tag_row = lax.broadcasted_iota(jnp.int32, (coarse_rows * SUB, LANES), 0) % SUB == 0

    def one_group(group, _):
        @pl.when(group + AHEAD < groups)
        def _():
            prepare(group + AHEAD)

        @pl.when(group > 0)
        def _():
            wait_halo(group)

        @pl.when(group == 0)
        def _():
            wait_halo(0)
            share_coefs()

        strips(group)
        march(group)
        high, low = split(sums[...])
        coarse = dot(high, pick[...]) + dot(low, pick[...])
        coarse = jnp.where(jnp.logical_and(tag_row, group == 0), tags[...], coarse)
        high, low = split(coarse)
        routed = dot(route[...], high) + dot(route[...], low)
        for k in range(ncol):
            outbound[group, k] = routed[k * CAP * SUB : (k + 1) * CAP * SUB]
        for step in range(1, ncol):
            to_owner(group, step).start()
        arrived[group, 0 : CAP * SUB, :] = outbound[group, col]
        return 0

    lax.fori_loop(0, groups, one_group, 0)

    for way in range(8):

        @pl.when(exists(way))
        def _(way=way):
            pltpu.make_async_copy(received[way], received[way], send_sem.at[way]).wait()

    sent_away = outbound.at[:, 1:ncol]
    pltpu.make_async_copy(sent_away, sent_away, out_sem.at[0]).wait()

    count = ncol * CAP
    filler = jnp.zeros((LANES - 2 * count, LANES), jnp.bfloat16)
    for group in range(groups):
        region = arrived.at[group, CAP * SUB : ncol * CAP * SUB, :]
        pltpu.make_async_copy(region, region, in_sem.at[group]).wait()
        if group == 0:
            named = arrived[0, pl.ds(0, count, stride=SUB), :]
            lines = lax.broadcasted_iota(jnp.int32, (count, LANES), 1).astype(jnp.float32) + 1.0
            picked = (named == lines).astype(jnp.float32)
            stack = jnp.concatenate(
                [picked, picked, jnp.zeros((LANES - 2 * count, LANES), jnp.float32)], 0
            )
            picker = stack.T[:PROWS].astype(jnp.bfloat16)
        for place in range(group * SUB, (group + 1) * SUB):
            if place >= lead:
                high, low = split(arrived[group, pl.ds(place % SUB, count, stride=SUB), :])
                parent[place - lead] = dot(picker, jnp.concatenate([high, low, filler], 0))


def finish(dims, nest, parent, nest_hbm, parent_hbm, store_sem):
    fields, levels, tile_rows = dims
    planes = fields * levels
    lead = round_up(planes + 1, SUB) - planes
    whole = pltpu.make_async_copy(parent, parent_hbm, store_sem.at[1])
    whole.start()
    for p in range(planes):
        pltpu.make_async_copy(
            nest.at[:, lead + p, :],
            nest_hbm.at[p * tile_rows : (p + 1) * tile_rows, :],
            store_sem.at[0],
        ).start()
    pltpu.make_async_copy(nest_hbm, nest_hbm, store_sem.at[0]).wait()
    whole.wait()


def shards(adjoint_field, advect_x, advect_y, diffusion, zone_cells, feedback_dest, feedback_slot):
    fields, levels, tile_rows, tile_cols = adjoint_field.shape
    planes = fields * levels
    tiles = tile_cols // LANES
    ncol = lax.axis_size("col")
    padded = round_up(planes + 1, SUB)
    groups = padded // SUB
    orders = variants_of(groups, levels)
    thirds = tile_rows * PAIR // LANES
    coarse_rows = tile_rows // 3
    wide = tiles * SUB
    f32 = jnp.float32
    vmem = pltpu.VMEM
    dma = pltpu.SemaphoreType.DMA
    smem_spec = pl.BlockSpec(memory_space=pltpu.SMEM)
    any_spec = pl.BlockSpec(memory_space=pl.ANY)
    vmem_spec = pl.BlockSpec(memory_space=pltpu.VMEM)
    own = (tile_rows, padded, tile_cols)
    level_own = (tile_rows, orders * SUB, tile_cols)
    halo_rows = ((groups + 1) * 2 * ITERS * wide, LANES)
    halo_cols = ((groups + 1) * thirds * SUB, LANES)
    halo_corner = (groups + 1) * 2 * SUB
    nest, parent = pl.pallas_call(
        functools.partial(kernel, (fields, levels, tile_rows, tiles)),
        out_shape=[
            pltpu.VMEM(own, f32),
            pltpu.VMEM((planes, PROWS, LANES), f32),
        ],
        in_specs=[smem_spec] * 3 + [any_spec] * 4,
        out_specs=[vmem_spec] * 2,
        scratch_shapes=[
            vmem((groups, ncol * CAP * SUB, LANES), f32),
            vmem(own, f32),
            vmem(own, f32),
            vmem(level_own, f32),
            vmem(level_own, f32),
            vmem((tile_rows, LANES), f32),
            vmem((tile_rows * wide, LANES), f32),
            vmem((tile_rows * wide, LANES), f32),
            vmem((coarse_rows * SUB, tiles * LANES), f32),
            vmem((tiles * LANES, LANES), jnp.bfloat16),
            vmem((ncol * CAP * SUB, coarse_rows * SUB), jnp.bfloat16),
            vmem((coarse_rows * SUB, LANES), f32),
            vmem((groups, ncol, CAP * SUB, LANES), f32),
        ]
        + [vmem(halo_rows, f32)] * 4
        + [vmem((2 * halo_cols[0], LANES), f32)]
        + [vmem(halo_cols, f32)] * 4
        + [
            vmem((4, halo_corner, LANES), f32),
            vmem((groups, 2, 2 * ITERS * wide, LANES), f32),
            vmem((groups, 2, 2 * (thirds + 1) * SUB, LANES), f32),
            vmem((ITERS, (thirds + 1) * SUB, LANES), f32),
            vmem((ITERS - 1, (tile_rows + 2 * ITERS) * wide, LANES), f32),
            dma((4 * groups,)),
            dma((8,)),
            dma((8 * groups,)),
            dma((1,)),
            dma((groups,)),
        ],
        compiler_params=pltpu.CompilerParams(
            collective_id=0, has_side_effects=True, vmem_limit_bytes=60 * 1024 * 1024
        ),
    )(
        zone_cells,
        feedback_dest.reshape(-1),
        feedback_slot.reshape(-1),
        adjoint_field.reshape(planes * tile_rows, tile_cols),
        diffusion.reshape(planes * tile_rows, tile_cols),
        advect_x.reshape(levels * tile_rows, tile_cols),
        advect_y.reshape(levels * tile_rows, tile_cols),
    )
    nest, parent = pl.pallas_call(
        functools.partial(finish, (fields, levels, tile_rows)),
        out_shape=(
            jax.ShapeDtypeStruct((planes * tile_rows, tile_cols), f32),
            jax.ShapeDtypeStruct((planes, PROWS, LANES), f32),
        ),
        in_specs=[vmem_spec] * 2,
        out_specs=(any_spec, any_spec),
        scratch_shapes=[dma((2,))],
        compiler_params=pltpu.CompilerParams(vmem_limit_bytes=16 * 1024 * 1024),
    )(nest, parent)
    return (
        nest.reshape(adjoint_field.shape),
        parent.reshape(fields, levels, PROWS, LANES),
    )


def solution(mesh):
    placed = (
        P(None, None, "row", "col"),
        P(None, "row", "col"),
        P(None, "row", "col"),
        P(None, None, "row", "col"),
        P(),
        P("col", "row", None),
        P("col", "row", None),
    )
    return jax.shard_map(
        shards,
        mesh=mesh,
        in_specs=placed,
        out_specs=(P(None, None, "row", "col"), P(None, None, "row", "col")),
        check_vma=False,
    )
```

```python
import functools
import math

import jax
import jax.numpy as jnp
from jax import lax
from jax.experimental import pallas as pl
from jax.experimental.pallas import tpu as pltpu
from jax.sharding import PartitionSpec as P

ITERS = 3
PROWS = 80
CAP = 2
LANES = 128
SUB = 8
PACK = 4
PAIR = 2 * PACK
AHEAD = 3
SLOTS = LANES // PAIR
MESH = pl.DeviceIdType.MESH
DIRS = ((-1, 0), (1, 0), (0, 1), (0, -1), (-1, 1), (-1, -1), (1, 1), (1, -1))
NORTH, SOUTH, EAST, WEST, NE, NW, SE, SW = range(8)
OPPOSITE = (SOUTH, NORTH, WEST, EAST, SW, SE, NW, NE)
GREETED = (NORTH, SOUTH, NE, NW, SE, SW)


def round_up(value, step):
    return -(-value // step) * step


def split(values):
    high = values.astype(jnp.bfloat16)
    return high, (values - high.astype(jnp.float32)).astype(jnp.bfloat16)


def dot(left, right):
    return jnp.dot(left, right, preferred_element_type=jnp.float32)


def variants_of(groups, levels):
    return min(groups, levels // math.gcd(levels, SUB))


def kernel(
    dims,
    zone_ref,
    dest_ref,
    slot_ref,
    field_hbm,
    spread_hbm,
    along_x_hbm,
    along_y_hbm,
    nest,
    parent,
    arrived,
    field,
    spread,
    along_x,
    along_y,
    ramps,
    keep,
    weigh,
    sums,
    pick,
    route,
    tags,
    outbound,
    rows_n,
    rows_s,
    got_n,
    got_s,
    slab,
    msg_e,
    msg_w,
    corner_n,
    corner_s,
    got_e,
    got_w,
    got_corner,
    halo_coef,
    edge_coef,
    edges,
    between,
    load_sem,
    send_sem,
    recv_sem,
    out_sem,
    in_sem,
):
    fields, levels, tile_rows, tiles = dims
    planes = fields * levels
    padded = round_up(planes + 1, SUB)
    groups, lead = padded // SUB, padded - planes
    wide = tiles * SUB
    per = 2 * ITERS * wide
    row, col = lax.axis_index("row"), lax.axis_index("col")
    nrow, ncol = lax.axis_size("row"), lax.axis_size("col")
    coarse_rows = tile_rows // 3

    def exists(way):
        down, over = DIRS[way]
        conditions = []
        if down < 0:
            conditions.append(row > 0)
        if down > 0:
            conditions.append(row < nrow - 1)
        if over < 0:
            conditions.append(col > 0)
        if over > 0:
            conditions.append(col < ncol - 1)
        return functools.reduce(jnp.logical_and, conditions)

    def device(way):
        return (row + DIRS[way][0], col + DIRS[way][1])

    def aligned(value):
        return value if isinstance(value, int) else pl.multiple_of(value, SUB)

    orders = variants_of(groups, levels)
    thirds = tile_rows // SLOTS
    strip = thirds * 2 * SUB
    arrays = ((field_hbm, field), (spread_hbm, spread), (along_x_hbm, along_x), (along_y_hbm, along_y))

    def load_group(group):
        for place in range(group * SUB, (group + 1) * SUB):
            for n, (source, target) in enumerate(arrays):
                if n < 2 and place < lead or n >= 2 and group >= orders:
                    continue
                number = place - lead if n < 2 else (place - lead) % levels
                pltpu.make_async_copy(
                    source.at[number * tile_rows : (number + 1) * tile_rows, :],
                    target.at[:, place, :],
                    load_sem.at[group * len(arrays) + n],
                ).start()

    def wait_load(group, n):
        target = arrays[n][1]
        if isinstance(group, int):
            first = max(group * SUB, lead) if n < 2 else group * SUB
            region = target.at[:, first : (group + 1) * SUB, :]
        else:
            region = target.at[:, pl.ds(aligned(group * SUB), SUB), :]
        pltpu.make_async_copy(region, region, load_sem.at[group * len(arrays) + n]).wait()

    load_group(0)

    barrier = pltpu.get_barrier_semaphore()
    for way in GREETED:

        @pl.when(exists(way))
        def _(way=way):
            pl.semaphore_signal(barrier, inc=1, device_id=device(way), device_id_type=MESH)

    for step in range(1, ncol):
        pl.semaphore_signal(
            barrier, inc=1, device_id=(row, lax.rem(col + step, ncol)), device_id_type=MESH
        )

    lane = lax.broadcasted_iota(jnp.int32, (SUB, LANES), 1)
    block = lane // PAIR
    lane_wide = lax.broadcasted_iota(jnp.int32, (wide, LANES), 1)
    lane_strip = lax.broadcasted_iota(jnp.int32, ((thirds + 1) * SUB, LANES), 1)
    inner = lane_strip % PAIR

    for ref in (field, spread):
        ref[:, 0:lead, :] = jnp.zeros((tile_rows, lead, tiles * LANES), jnp.float32)

    received = {NORTH: got_n, SOUTH: got_s, EAST: got_e, WEST: got_w}
    for place, way in enumerate((NE, NW, SE, SW)):
        received[way] = got_corner.at[place]
    for way in range(8):

        @pl.when(jnp.logical_not(exists(way)))
        def _(way=way):
            received[way][...] = jnp.zeros(received[way].shape, jnp.float32)

    def planes_at(ref, t, group, r):
        at = group * SUB if isinstance(group, int) else pl.multiple_of(group * SUB, SUB)
        return ref[r, pl.ds(at, SUB), t * LANES : (t + 1) * LANES]

    def both_edges(first, last, spot_):
        return pltpu.roll(jnp.where(lane < PACK, first, last), PAIR * spot_ + PACK, 1)

    def gather_rows(source, group, at):
        for i in range(ITERS):
            for t in range(tiles):
                place = pl.ds(at + i * wide + t * SUB, SUB)
                rows_n[place, :] = planes_at(source, t, group, i)
                rows_s[place, :] = planes_at(source, t, group, tile_rows - ITERS + i)

    def put_columns(pieces, group, at):
        for n, source in enumerate(pieces):
            for third in range(thirds):
                value = jnp.zeros((SUB, LANES), jnp.float32)
                for spot_ in range(SLOTS):
                    r = third * SLOTS + spot_
                    moved = both_edges(
                        planes_at(source, 0, group, r),
                        planes_at(source, tiles - 1, group, r),
                        spot_,
                    )
                    value = jnp.where(block == spot_, moved, value)
                slab[pl.ds(at + (2 * third + n) * SUB, SUB), :] = value

    def fill_tables():
        def ramp(position, count, low_zone, high_zone):
            shape = position.shape
            scale_low = jnp.full(shape, (low_zone + 1).astype(jnp.float32))
            scale_high = jnp.full(shape, (high_zone + 1).astype(jnp.float32))
            lower = jnp.maximum(low_zone - position, 0).astype(jnp.float32) / scale_low
            upper = jnp.maximum(high_zone - (count - 1 - position), 0).astype(jnp.float32) / scale_high
            return jnp.maximum(lower, upper)

        row_index = row * tile_rows + lax.broadcasted_iota(jnp.int32, (tile_rows, LANES), 0)
        ramps[...] = ramp(row_index, tile_rows * nrow, zone_ref[0], zone_ref[1])
        tile_index = lax.broadcasted_iota(jnp.int32, (wide, LANES), 0) // SUB
        weight_cols = ramp(
            (col * tiles + tile_index) * LANES + lane_wide,
            tiles * LANES * ncol,
            zone_ref[2],
            zone_ref[3],
        )

        def weights(r, _):
            across = jnp.broadcast_to(ramps[pl.ds(r, 1), :], (wide, LANES))
            relaxation = jnp.maximum(across, weight_cols)
            at = pl.multiple_of(r * wide, SUB)
            keep[pl.ds(at, wide), :] = 1.0 - relaxation
            weigh[pl.ds(at, wide), :] = (1.0 - relaxation) / 9.0 + relaxation
            return 0

        lax.fori_loop(0, tile_rows, weights, 0, unroll=4)

        fine = lax.broadcasted_iota(jnp.int32, (tiles * LANES, LANES), 0)
        name = lax.broadcasted_iota(jnp.int32, (tiles * LANES, LANES), 1)
        pick[...] = (fine // 3 == name).astype(jnp.float32).astype(jnp.bfloat16)

        dests = [dest_ref[g] for g in range(coarse_rows)]
        from_lane = lax.broadcasted_iota(jnp.int32, (SUB, coarse_rows * SUB), 1)
        spot = jnp.zeros((SUB, coarse_rows * SUB), jnp.int32)
        for g in range(coarse_rows):
            rank = jnp.int32(0)
            for before in range(g):
                rank = rank + jnp.where(dests[before] == dests[g], 1, 0)
            spot = jnp.where(from_lane // SUB == g, dests[g] * CAP + rank, spot)
            tags[g * SUB : (g + 1) * SUB, :] = jnp.full(
                (SUB, LANES), (slot_ref[g] + 1).astype(jnp.float32)
            )
        same = from_lane % SUB == lax.broadcasted_iota(jnp.int32, (SUB, coarse_rows * SUB), 0)
        spot = jnp.where(same, spot, -1)
        for k in range(0, ncol * CAP, 2):
            pair = jnp.concatenate(
                [(spot == k).astype(jnp.float32), (spot == k + 1).astype(jnp.float32)], 0
            )
            route[k * SUB : (k + 2) * SUB, :] = pair.astype(jnp.bfloat16)

    first_half = lane % PAIR < PACK

    def put_messages(part):
        base, to = aligned(part * strip), aligned(part * thirds * SUB)
        units = [
            slab[pl.ds(base + (2 * third + n) * SUB, SUB), :]
            for n in range(2)
            for third in range(thirds)
        ]
        for i in range(thirds):
            one, two = units[2 * i], units[2 * i + 1]
            place = pl.ds(to + i * SUB, SUB)
            msg_e[place, :] = jnp.where(first_half, one, pltpu.roll(two, PACK, 1))
            msg_w[place, :] = jnp.where(first_half, pltpu.roll(one, LANES - PACK, 1), two)

        place = pl.ds(aligned(part * SUB), SUB)
        low = lane < LANES // 2
        one, two = units[0], units[thirds]
        corner_n[place, :] = jnp.where(low, one, pltpu.roll(two, LANES // 2, 1))
        one, two = units[thirds - 1], units[2 * thirds - 1]
        corner_s[place, :] = jnp.where(low, pltpu.roll(two, LANES // 2, 1), one)

    sources = {NORTH: rows_n, SOUTH: rows_s, EAST: msg_e, WEST: msg_w}
    for way in (NE, NW):
        sources[way] = corner_n
    for way in (SE, SW):
        sources[way] = corner_s

    def remote(way, group, arriving=False):
        sent = OPPOSITE[way] if arriving else way
        back = OPPOSITE[sent]
        whole = per if sent < 2 else thirds * SUB if sent < 4 else SUB
        if isinstance(group, int) and group == 0:
            place = pl.ds(0, 2 * whole)
        else:
            place = pl.ds(aligned((group + 1) * whole), whole)
        return pltpu.make_async_remote_copy(
            src_ref=sources[sent].at[place, :],
            dst_ref=received[back].at[place, :],
            send_sem=send_sem.at[sent],
            recv_sem=recv_sem.at[group * 8 + back],
            device_id=device(way),
            device_id_type=MESH,
        )

    def greet():
        greeted = jnp.int32(ncol - 1)
        for way in GREETED:
            greeted = greeted + exists(way).astype(jnp.int32)
        pl.semaphore_wait(barrier, greeted)

    def send_halo(group):
        put_columns((field, spread), group, aligned((group + 1) * strip))
        put_messages(group + 1)
        if isinstance(group, int) and group == 0:
            greet()
        for way in (EAST, WEST, NE, NW, SE, SW):

            @pl.when(exists(way))
            def _(way=way):
                remote(way, group).start()

        if isinstance(group, int) and group == 0:
            gather_rows(along_x, 0, 0)
            gather_rows(along_y, 0, ITERS * wide)
        at = aligned((group + 1) * per)
        gather_rows(field, group, at)
        gather_rows(spread, group, at + ITERS * wide)
        for way in (NORTH, SOUTH):

            @pl.when(exists(way))
            def _(way=way):
                remote(way, group).start()

    def prepare(group):
        for n in range(2):
            wait_load(group, n)
        if isinstance(group, int):
            if group < orders:
                for n in range(2, len(arrays)):
                    wait_load(group, n)
        else:

            @pl.when(group < orders)
            def _():
                for n in range(2, len(arrays)):
                    wait_load(group, n)

        send_halo(group)

    fill_tables()
    for n in range(len(arrays)):
        wait_load(0, n)
    put_columns((along_x, along_y), 0, 0)
    put_messages(0)
    send_halo(0)
    for later in range(1, groups):
        load_group(later)
    for later in range(1, min(AHEAD, groups)):
        prepare(later)

    def strip_of(array, base, message_base, corner_base, group_base):
        halo = jnp.zeros((SUB, LANES), jnp.float32)
        for got, first_slot in ((got_n, SLOTS - ITERS), (got_s, 0)):
            for i in range(ITERS):
                at = group_base + (array * ITERS + i) * wide
                moved = both_edges(
                    got[pl.ds(at, SUB), :],
                    got[pl.ds(at + (tiles - 1) * SUB, SUB), :],
                    first_slot + i,
                )
                halo = jnp.where(block == first_slot + i, moved, halo)

        def unpacked(got, side, third):
            pair, second = divmod(array * thirds + third, 2)
            value = got[pl.ds(message_base + pair * SUB, SUB), :]
            if side == 0:
                return value if second else pltpu.roll(value, PACK, 1)
            return pltpu.roll(value, LANES - PACK, 1) if second else value

        parts = [slab[pl.ds(base + (2 * third + array) * SUB, SUB), :] for third in range(thirds)]
        own = jnp.concatenate(parts + [halo], 0)
        out = []
        for side, got in enumerate((got_e, got_w)):
            corner = pl.ds(corner_base, SUB)
            above, below = got_corner[side, corner, :], got_corner[2 + side, corner, :]
            last = jnp.where(lane < LANES // 2, below, above)
            if array == 1:
                last = pltpu.roll(jnp.where(lane < LANES // 2, above, below), LANES // 2, 1)
            last = jnp.where(
                jnp.logical_or(block >= SLOTS - ITERS, block < ITERS), last, jnp.zeros_like(last)
            )
            parts = [unpacked(got, side, third) for third in range(thirds)]
            other = jnp.concatenate(parts + [last], 0)
            west, east = (own, other) if side == 0 else (other, own)
            out.append(jnp.where(inner < PACK, west, east))
        return out

    def variants(value):
        sub = lax.broadcasted_iota(jnp.int32, (SUB, LANES), 0)
        out = []
        for group in range(groups):
            shift = (group * SUB) % levels
            if shift == 0:
                out.append(value)
            else:
                out.append(
                    jnp.where(
                        sub + shift < SUB,
                        pltpu.roll(value, SUB - shift, 0),
                        pltpu.roll(value, levels - shift, 0),
                    )
                )
        return out

    def wait_halo(group):
        for way in range(8):

            @pl.when(exists(way))
            def _(way=way):
                remote(way, group, True).wait_recv()

    def share_coefs():
        for which, got in enumerate((got_n, got_s)):

            def one(n, _, got=got, which=which):
                at = pl.multiple_of(n * SUB, SUB)
                for group, value in enumerate(variants(got[pl.ds(at, SUB), :])):
                    halo_coef[group, which, pl.ds(at, SUB), :] = value
                return 0

            lax.fori_loop(0, per // SUB, one, 0, unroll=6)
        for array in range(2):
            for side, value in enumerate(strip_of(array, 0, 0, 0, 0)):
                for third in range(thirds + 1):
                    at = (array * (thirds + 1) + third) * SUB
                    part = value[third * SUB : (third + 1) * SUB]
                    for group, moved in enumerate(variants(part)):
                        edge_coef[group, side, at : at + SUB, :] = moved

    def products(v, d, along, across):
        w = 0.5 * v
        p, x, y = d * v, along * w, across * w
        return v - 4.0 * p, p + x, p - x, p + y, p - y

    def next_rows(value):
        moved = pltpu.roll(value, PAIR, 1)
        carried = jnp.concatenate([moved[thirds * SUB :], moved[: thirds * SUB]], 0)
        return jnp.where(lane_strip < PAIR, carried, moved)

    def previous_rows(value):
        moved = pltpu.roll(value, LANES - PAIR, 1)
        carried = jnp.concatenate([moved[SUB:], moved[:SUB]], 0)
        return jnp.where(lane_strip >= LANES - PAIR, carried, moved)

    def strips(group):
        base = pl.multiple_of((group + 1) * strip, SUB)
        message_base = pl.multiple_of((group + 1) * thirds * SUB, SUB)
        corner_base = pl.multiple_of((group + 1) * SUB, SUB)
        group_base = pl.multiple_of((group + 1) * per, SUB)
        fields_now = strip_of(0, base, message_base, corner_base, group_base)
        spreads = strip_of(1, base, message_base, corner_base, group_base)
        count = (thirds + 1) * SUB
        flux = []
        for side in range(2):
            now, d = fields_now[side], spreads[side]
            hx = edge_coef[group, side, 0:count, :]
            hy = edge_coef[group, side, count : 2 * count, :]
            flux.append([])
            for sweep in range(ITERS):
                center, up, down, right, left = products(now, d, hx, hy)
                flux[side].append(right if side == 0 else left)
                if sweep < ITERS - 1:
                    now = (
                        center
                        + previous_rows(up)
                        + next_rows(down)
                        + (pltpu.roll(right, LANES - 1, 1) + pltpu.roll(left, 1, 1))
                    )
        for sweep in range(ITERS):
            edges[sweep] = jnp.where(
                inner == PACK, flux[0][sweep], pltpu.roll(flux[1][sweep], 2, 1)
            )

    def march(group):
        order = lax.rem(group, orders)
        at_last, at_first = lane_wide == LANES - 1, lane_wide == 0

        def row_of(ref, r, which):
            return jnp.concatenate([planes_at(ref, t, which, r) for t in range(tiles)], 0)

        def coefs(r):
            if 0 <= r < tile_rows:
                return (
                    row_of(spread, r, group),
                    row_of(along_x, r, order),
                    row_of(along_y, r, order),
                )
            which, i = (0, r + ITERS) if r < 0 else (1, r - tile_rows)
            base = pl.multiple_of((group + 1) * per, SUB)
            d = (got_n, got_s)[which][pl.ds(base + (ITERS + i) * wide, wide), :]
            along = halo_coef[group, which, i * wide : (i + 1) * wide, :]
            across = halo_coef[group, which, (ITERS + i) * wide : (ITERS + i + 1) * wide, :]
            return d, along, across

        def value(sweep, r):
            if sweep > 0:
                return between[sweep - 1, (r + ITERS) * wide : (r + ITERS + 1) * wide, :]
            if 0 <= r < tile_rows:
                return row_of(field, r, group)
            which, i = (0, r + ITERS) if r < 0 else (1, r - tile_rows)
            base = pl.multiple_of((group + 1) * per, SUB)
            return (got_n, got_s)[which][pl.ds(base + i * wide, wide), :]

        def lateral(right, left, sweep, r):
            part, spot_ = divmod(r % ((thirds + 1) * SLOTS), SLOTS)
            beyond = pltpu.roll(
                edges[sweep, part * SUB : (part + 1) * SUB, :],
                LANES - 1 - PACK - PAIR * spot_,
                1,
            )
            right, left = pltpu.roll(right, LANES - 1, 1), pltpu.roll(left, 1, 1)
            from_right = jnp.concatenate([right[SUB:], beyond], 0)
            from_left = jnp.concatenate([beyond, left[: wide - SUB]], 0)
            return jnp.where(at_last, from_right, right) + jnp.where(at_first, from_left, left)

        def finish_row(r, v):
            at = r * wide if isinstance(r, int) else pl.multiple_of(r * wide, SUB)
            out = keep[pl.ds(at, wide), :] * v
            for t in range(tiles):
                place = pl.ds(pl.multiple_of(group * SUB, SUB), SUB)
                nest[r, place, t * LANES : (t + 1) * LANES] = out[t * SUB : (t + 1) * SUB]
            return weigh[pl.ds(at, wide), :] * v

        def put_sum(g, value):
            at = g * SUB if isinstance(g, int) else pl.multiple_of(g * SUB, SUB)
            for t in range(tiles):
                sums[pl.ds(at, SUB), t * LANES : (t + 1) * LANES] = value[t * SUB : (t + 1) * SUB]

        total = None
        for sweep in range(ITERS):
            reach = ITERS - 1 - sweep
            base, sideways, down = None, None, None
            for r in range(-reach - 1, tile_rows + reach + 1):
                v = value(sweep, r)
                d, along, across = coefs(r)
                if r == -reach - 1:
                    down = d * v - along * (0.5 * v)
                    continue
                if r == tile_rows + reach:
                    up = d * v + along * (0.5 * v)
                else:
                    center, up, below, right, left = products(v, d, along, across)
                done = r - 1
                if done >= -reach:
                    result = (base + up) + sideways
                    if sweep < ITERS - 1:
                        between[sweep, (done + ITERS) * wide : (done + ITERS + 1) * wide, :] = result
                    else:
                        term = finish_row(done, result)
                        total = term if done % 3 == 0 else total + term
                        if done % 3 == 2:
                            put_sum(done // 3, total)
                if r < tile_rows + reach:
                    base = center + down
                    sideways = lateral(right, left, sweep, r)
                    down = below

    def to_owner(group, step):
        owner = lax.rem(col + step, ncol)
        rows = CAP * SUB
        return pltpu.make_async_remote_copy(
            src_ref=outbound.at[group, owner],
            dst_ref=arrived.at[group, pl.ds(step * rows, rows), :],
            send_sem=out_sem.at[0],
            recv_sem=in_sem.at[group],
            device_id=(row, owner),
            device_id_type=MESH,
        )

    tag_row = lax.broadcasted_iota(jnp.int32, (coarse_rows * SUB, LANES), 0) % SUB == 0

    def one_group(group, _):
        @pl.when(group + AHEAD < groups)
        def _():
            prepare(group + AHEAD)

        @pl.when(group > 0)
        def _():
            wait_halo(group)

        @pl.when(group == 0)
        def _():
            wait_halo(0)
            share_coefs()

        strips(group)
        march(group)
        high, low = split(sums[...])
        coarse = dot(high, pick[...]) + dot(low, pick[...])
        coarse = jnp.where(jnp.logical_and(tag_row, group == 0), tags[...], coarse)
        high, low = split(coarse)
        routed = dot(route[...], high) + dot(route[...], low)
        for k in range(ncol):
            outbound[group, k] = routed[k * CAP * SUB : (k + 1) * CAP * SUB]
        for step in range(1, ncol):
            to_owner(group, step).start()
        arrived[group, 0 : CAP * SUB, :] = outbound[group, col]
        return 0

    lax.fori_loop(0, groups, one_group, 0)

    for way in range(8):

        @pl.when(exists(way))
        def _(way=way):
            pltpu.make_async_copy(received[way], received[way], send_sem.at[way]).wait()

    sent_away = outbound.at[:, 1:ncol]
    pltpu.make_async_copy(sent_away, sent_away, out_sem.at[0]).wait()

    count = ncol * CAP
    filler = jnp.zeros((LANES - 2 * count, LANES), jnp.bfloat16)
    for group in range(groups):
        region = arrived.at[group, CAP * SUB : ncol * CAP * SUB, :]
        pltpu.make_async_copy(region, region, in_sem.at[group]).wait()
        if group == 0:
            named = arrived[0, pl.ds(0, count, stride=SUB), :]
            lines = lax.broadcasted_iota(jnp.int32, (count, LANES), 1).astype(jnp.float32) + 1.0
            picked = (named == lines).astype(jnp.float32)
            stack = jnp.concatenate(
                [picked, picked, jnp.zeros((LANES - 2 * count, LANES), jnp.float32)], 0
            )
            picker = stack.T[:PROWS].astype(jnp.bfloat16)
        for place in range(group * SUB, (group + 1) * SUB):
            if place >= lead:
                high, low = split(arrived[group, pl.ds(place % SUB, count, stride=SUB), :])
                parent[place - lead] = dot(picker, jnp.concatenate([high, low, filler], 0))


def finish(dims, nest, parent, nest_hbm, parent_hbm, store_sem):
    fields, levels, tile_rows = dims
    planes = fields * levels
    lead = round_up(planes + 1, SUB) - planes
    whole = pltpu.make_async_copy(parent, parent_hbm, store_sem.at[1])
    whole.start()
    for p in range(planes):
        pltpu.make_async_copy(
            nest.at[:, lead + p, :],
            nest_hbm.at[p * tile_rows : (p + 1) * tile_rows, :],
            store_sem.at[0],
        ).start()
    pltpu.make_async_copy(nest_hbm, nest_hbm, store_sem.at[0]).wait()
    whole.wait()


def shards(adjoint_field, advect_x, advect_y, diffusion, zone_cells, feedback_dest, feedback_slot):
    fields, levels, tile_rows, tile_cols = adjoint_field.shape
    planes = fields * levels
    tiles = tile_cols // LANES
    ncol = lax.axis_size("col")
    padded = round_up(planes + 1, SUB)
    groups = padded // SUB
    orders = variants_of(groups, levels)
    thirds = tile_rows * PAIR // LANES
    coarse_rows = tile_rows // 3
    wide = tiles * SUB
    f32 = jnp.float32
    vmem = pltpu.VMEM
    dma = pltpu.SemaphoreType.DMA
    smem_spec = pl.BlockSpec(memory_space=pltpu.SMEM)
    any_spec = pl.BlockSpec(memory_space=pl.ANY)
    vmem_spec = pl.BlockSpec(memory_space=pltpu.VMEM)
    own = (tile_rows, padded, tile_cols)
    level_own = (tile_rows, orders * SUB, tile_cols)
    halo_rows = ((groups + 1) * 2 * ITERS * wide, LANES)
    halo_cols = ((groups + 1) * thirds * SUB, LANES)
    halo_corner = (groups + 1) * SUB
    nest, parent = pl.pallas_call(
        functools.partial(kernel, (fields, levels, tile_rows, tiles)),
        out_shape=[
            pltpu.VMEM(own, f32),
            pltpu.VMEM((planes, PROWS, LANES), f32),
        ],
        in_specs=[smem_spec] * 3 + [any_spec] * 4,
        out_specs=[vmem_spec] * 2,
        scratch_shapes=[
            vmem((groups, ncol * CAP * SUB, LANES), f32),
            vmem(own, f32),
            vmem(own, f32),
            vmem(level_own, f32),
            vmem(level_own, f32),
            vmem((tile_rows, LANES), f32),
            vmem((tile_rows * wide, LANES), f32),
            vmem((tile_rows * wide, LANES), f32),
            vmem((coarse_rows * SUB, tiles * LANES), f32),
            vmem((tiles * LANES, LANES), jnp.bfloat16),
            vmem((ncol * CAP * SUB, coarse_rows * SUB), jnp.bfloat16),
            vmem((coarse_rows * SUB, LANES), f32),
            vmem((groups, ncol, CAP * SUB, LANES), f32),
        ]
        + [vmem(halo_rows, f32)] * 4
        + [vmem((2 * halo_cols[0], LANES), f32)]
        + [vmem(halo_cols, f32)] * 2
        + [vmem((halo_corner, LANES), f32)] * 2
        + [vmem(halo_cols, f32)] * 2
        + [
            vmem((4, halo_corner, LANES), f32),
            vmem((groups, 2, 2 * ITERS * wide, LANES), f32),
            vmem((groups, 2, 2 * (thirds + 1) * SUB, LANES), f32),
            vmem((ITERS, (thirds + 1) * SUB, LANES), f32),
            vmem((ITERS - 1, (tile_rows + 2 * ITERS) * wide, LANES), f32),
            dma((4 * groups,)),
            dma((8,)),
            dma((8 * groups,)),
            dma((1,)),
            dma((groups,)),
        ],
        compiler_params=pltpu.CompilerParams(
            collective_id=0, has_side_effects=True, vmem_limit_bytes=60 * 1024 * 1024
        ),
    )(
        zone_cells,
        feedback_dest.reshape(-1),
        feedback_slot.reshape(-1),
        adjoint_field.reshape(planes * tile_rows, tile_cols),
        diffusion.reshape(planes * tile_rows, tile_cols),
        advect_x.reshape(levels * tile_rows, tile_cols),
        advect_y.reshape(levels * tile_rows, tile_cols),
    )
    nest, parent = pl.pallas_call(
        functools.partial(finish, (fields, levels, tile_rows)),
        out_shape=(
            jax.ShapeDtypeStruct((planes * tile_rows, tile_cols), f32),
            jax.ShapeDtypeStruct((planes, PROWS, LANES), f32),
        ),
        in_specs=[vmem_spec] * 2,
        out_specs=(any_spec, any_spec),
        scratch_shapes=[dma((2,))],
        compiler_params=pltpu.CompilerParams(vmem_limit_bytes=16 * 1024 * 1024),
    )(nest, parent)
    return (
        nest.reshape(adjoint_field.shape),
        parent.reshape(fields, levels, PROWS, LANES),
    )


def solution(mesh):
    placed = (
        P(None, None, "row", "col"),
        P(None, "row", "col"),
        P(None, "row", "col"),
        P(None, None, "row", "col"),
        P(),
        P("col", "row", None),
        P("col", "row", None),
    )
    return jax.shard_map(
        shards,
        mesh=mesh,
        in_specs=placed,
        out_specs=(P(None, None, "row", "col"), P(None, None, "row", "col")),
        check_vma=False,
    )
```
